128 devices in a mesh: row: 16 (over z_lo, y, core), col: 8 (over z_hi, x).
Axes of the slice: x: 4, y: 4, z: 4 (z_hi: 2, z_lo: 2; z = z_hi * 2 + z_lo), core: 2. Of those that a mesh axis runs over, the one named last changes fastest.
Arguments:
- a_values: float32 [8192, 8192], P('row', 'col'), may hold values from -6 to 6
- a_mask: int32 [64, 64], P('row', 'col'), may hold values from 0 to 1, as said below
- b_values: float32 [8192, 8192], P('row', 'col'), may hold values from -0.5 to 0.5
- b_mask: int32 [64, 64], P('row', 'col'), may hold values from 0 to 1, as said below
- keep: int32 [64, 64, 64], P('row', None, 'col'), may hold values from 0 to 1, as said below
Outputs:
- product: float32 [8192, 8192], P('row', 'col')
The draws below stay inside these ranges and needn't reach their ends.
Inputs may be any that keep to these rules, and one draw needn't show every extreme that they name: `keep`: 0 means the triple is filtered out, 1 that it counts. `a_mask`: 1 means the block is stored; on one device at most 20 blocks are stored, and some device holds exactly 20. `b_mask`: 1 means the block is stored; on one device at most 20 blocks are stored, and some device holds exactly 20.
All inputs are finite; a program needn't handle non-finite values.
Results may differ from the reference program's by a relative error of at most 0.000071.
Values sent between devices are 32-bit elements; how exact they have to be, the bound alone decides.
No kernel may reach another device: no remote copies, remote signals or barrier semaphores. Data moves between devices by JAX's collectives and lax.ppermute only.
A program may use at most 384 MiB of HBM per device.

```python
import jax
import jax.numpy as jnp
from jax import lax

BS = 128
IBR = 4
JBC = 8
KB = 64
IB = 64
JB = 64


def device_mask(key, grid_rows, grid_cols, block_rows, block_cols):
    slot_count = block_rows * block_cols
    devices = grid_rows * grid_cols
    largest = 5 * slot_count // 8
    lowest = max(1, slot_count // 8)
    highest = max(lowest, 5 * slot_count // 16)
    key_count, key_heavy, key_perm = jax.random.split(key, 3)
    counts = jax.random.randint(key_count, (devices,), lowest, highest + 1)
    heaviest = jax.random.randint(key_heavy, (), 0, devices)
    counts = jnp.where(jnp.arange(devices, dtype=jnp.int32) == heaviest, largest, counts)
    perm_keys = jax.random.split(key_perm, devices)
    rank_table = jax.vmap(lambda single: jax.random.permutation(single, slot_count))(perm_keys)
    stored = (rank_table < counts[:, None]).astype(jnp.int32)
    stored = stored.reshape(grid_rows, grid_cols, block_rows, block_cols)
    return jnp.transpose(stored, (0, 2, 1, 3)).reshape(grid_rows * block_rows, grid_cols * block_cols)


def draw_a_mask(key, part):
    grid_rows = IB // IBR
    grid_cols = JB // JBC
    return device_mask(jax.random.fold_in(key, 11), grid_rows, grid_cols, IBR, KB // grid_cols)


def draw_b_mask(key, part):
    grid_rows = IB // IBR
    grid_cols = JB // JBC
    return device_mask(jax.random.fold_in(key, 23), grid_rows, grid_cols, KB // grid_rows, JBC)


def draw_keep(key, part):
    grid_rows = IB // IBR
    grid_cols = JB // JBC
    key_level, key_heavy, key_bits = jax.random.split(jax.random.fold_in(key, 37), 3)
    levels = jax.random.randint(key_level, (grid_rows * grid_cols,), 1, 4)
    heaviest = jax.random.randint(key_heavy, (), 0, grid_rows * grid_cols)
    levels = jnp.where(jnp.arange(grid_rows * grid_cols, dtype=jnp.int32) == heaviest, 4, levels)
    levels = levels.reshape(grid_rows, grid_cols)
    values = jax.random.randint(key_bits, (grid_rows, IBR, KB, grid_cols, JBC), 0, 4)
    passed = (values < levels[:, None, None, :, None]).astype(jnp.int32)
    return passed.reshape(IB, KB, JB)


def block_levels(key, dims, cuts, low, high):
    def one(dim, parts):
        draws = jax.random.uniform(jax.random.fold_in(jax.random.fold_in(key, 6), dim), (parts,), jnp.float32, low / len(cuts), high / len(cuts))
        return jnp.repeat(jnp.exp(draws), dims[dim] // parts).reshape((-1,) + (1,) * (len(dims) - dim - 1))

    factor_of = one(*cuts[0])
    for cut in cuts[1:]:
        factor_of = factor_of * one(*cut)
    return factor_of


def gaussian(stream_key, dims, deviation, bound, cuts=(), held_as=jnp.bfloat16):
    array = jax.random.normal(stream_key, dims, jnp.float32) * deviation
    if len(cuts) > 0:
        array = block_levels(stream_key, dims, cuts, -0.22, 0.18) * array
    return jnp.clip(array, min=-bound, max=bound).astype(held_as)


def setup_inputs(seed: int = 0) -> dict:
    arg_keys = jax.random.split(jax.random.key(seed), 6)
    return {
        "a_values": gaussian(arg_keys[0], (IB * BS, KB * BS), 1.0, 6.0, ((0, 16), (1, 8)), jnp.float32),
        "a_mask": draw_a_mask(jax.random.fold_in(arg_keys[5], 71), 0),
        "b_values": gaussian(arg_keys[2], (KB * BS, JB * BS), BS ** -0.5, 0.5, ((0, 16), (1, 8)), jnp.float32),
        "b_mask": draw_b_mask(jax.random.fold_in(arg_keys[5], 71), 0),
        "keep": draw_keep(jax.random.fold_in(arg_keys[5], 71), 0),
    }


def reference(a_values, a_mask, b_values, b_mask, keep):
    row_blocks, inner_blocks = a_mask.shape
    col_blocks = b_mask.shape[1]
    width = a_values.shape[0] // row_blocks
    first = (a_values.reshape(row_blocks, width, inner_blocks, width) * a_mask.astype(jnp.float32)[:, None, :, None]).reshape(row_blocks * width, inner_blocks * width)
    second = (b_values.reshape(inner_blocks, width, col_blocks, width) * b_mask.astype(jnp.float32)[:, None, :, None]).reshape(inner_blocks * width, col_blocks * width)
    weights = jnp.repeat(keep.astype(jnp.float32), width, axis=1)

    def column(index):
        weight_col = lax.dynamic_index_in_dim(weights, index, 2, keepdims=False)
        masked = (first.reshape(row_blocks, width, inner_blocks * width) * weight_col[:, None, :]).reshape(row_blocks * width, inner_blocks * width)
        second_col = lax.dynamic_slice_in_dim(second, index * width, width, 1)
        return jnp.dot(masked, second_col, precision=lax.Precision.HIGHEST, preferred_element_type=jnp.float32)

    columns = lax.map(column, jnp.arange(col_blocks, dtype=jnp.int32))
    return jnp.transpose(columns, (1, 0, 2)).reshape(row_blocks * width, col_blocks * width)
```

```python
import functools

import jax
import jax.numpy as jnp
import numpy as np
from jax import lax
from jax.experimental import pallas as pl
from jax.experimental.pallas import tpu as pltpu
from jax.sharding import Mesh
from jax.sharding import PartitionSpec as P

W = 128
SLOTS = 20
DATA = SLOTS * W
ROWS = DATA + 8
HALF = DATA // 2
ROW = ("zl", "y", "core")
COL = ("zh", "x")


def pack_kernel(am_ref, bm_ref, a_ref, b_ref, am_tile, bm_tile, pa_ref, pb_ref, sem_a, sem_b, sem_m):
    tiles = (
        pltpu.make_async_copy(am_tile, pa_ref.at[pl.ds(DATA, 8), :], sem_m.at[0]),
        pltpu.make_async_copy(bm_tile, pb_ref.at[pl.ds(DATA, 8), :], sem_m.at[1]),
    )
    for tile in tiles:
        tile.start()

    def move(mask, src, dst, sem):
        rows, cols = mask.shape
        slot = jnp.int32(0)
        for r in range(rows):
            for c in range(cols):
                on = mask[r, c] != 0

                @pl.when(on)
                def _():
                    at = pl.multiple_of(slot * W, W)
                    pltpu.make_async_copy(
                        src.at[pl.ds(r * W, W), pl.ds(c * W, W)], dst.at[pl.ds(at, W), :], sem.at[r * cols + c]
                    ).start()

                slot = slot + on.astype(jnp.int32)

    def finish(mask, src, dst, sem):
        rows, cols = mask.shape
        for r in range(rows):
            for c in range(cols):

                @pl.when(mask[r, c] != 0)
                def _():
                    pltpu.make_async_copy(
                        src.at[pl.ds(r * W, W), pl.ds(c * W, W)], dst.at[pl.ds(0, W), :], sem.at[r * cols + c]
                    ).wait()

    move(am_ref, a_ref, pa_ref, sem_a)
    move(bm_ref, b_ref, pb_ref, sem_b)
    finish(am_ref, a_ref, pa_ref, sem_a)
    finish(bm_ref, b_ref, pb_ref, sem_b)
    for tile in tiles:
        tile.wait()


def pack(a_mask, b_mask, a_values, b_values, a_tile, b_tile):
    smem = pl.BlockSpec(memory_space=pltpu.SMEM)
    hbm = pl.BlockSpec(memory_space=pl.ANY)
    shape = jax.ShapeDtypeStruct((ROWS, W), jnp.float32)
    return pl.pallas_call(
        pack_kernel,
        out_shape=(shape, shape),
        in_specs=[smem, smem, hbm, hbm, hbm, hbm],
        out_specs=(hbm, hbm),
        scratch_shapes=[
            pltpu.SemaphoreType.DMA((32,)),
            pltpu.SemaphoreType.DMA((32,)),
            pltpu.SemaphoreType.DMA((2,)),
        ],
        name="pack",
    )(a_mask, b_mask, a_values, b_values, a_tile, b_tile)


def split(x):
    high = x.astype(jnp.bfloat16)
    low = (x - high.astype(jnp.float32)).astype(jnp.bfloat16)
    return high, low


def product_kernel(plan, where_ref, keep_ref, *refs):
    count = len(plan)
    pieces = refs[:count]
    out_ref, a_all, b_all, a_meta, b_meta, table, words, table_s, words_s, sem, sem_t = refs[count:]
    copies = []
    for n, (which, part) in enumerate(plan):
        at = where_ref[n]
        data, meta, step = (a_all, a_meta, 8) if which == "a" else (b_all, b_meta, 8)
        base = at * DATA
        piece = pieces[n]
        if part != "first":
            copies.append((piece.at[pl.ds(piece.shape[0] - 8, 8), :], meta.at[pl.ds(at * 8, 8), :]))
        if part == "whole":
            copies.append((piece.at[pl.ds(0, DATA), :], data.at[pl.ds(base, DATA), :]))
        elif part == "first":
            copies.append((piece, data.at[pl.ds(base, HALF), :]))
        else:
            copies.append((piece.at[pl.ds(0, HALF), :], data.at[pl.ds(base + HALF, HALF), :]))
    copies = [pltpu.make_async_copy(src, dst, sem.at[n]) for n, (src, dst) in enumerate(copies)]
    for copy in copies:
        copy.start()
    for copy in copies:
        copy.wait()

    k8 = lax.broadcasted_iota(jnp.int32, (8, W), 0)
    one = jnp.ones((8, W), jnp.int32)
    low = jnp.zeros((8, W), jnp.int32)
    high = jnp.zeros((8, W), jnp.int32)
    for c in range(8):
        a_slot = a_meta[pl.ds(c * 8, 8), :].astype(jnp.int32)
        b0 = b_meta[pl.ds(c * 16, 8), :].astype(jnp.int32)
        b1 = pltpu.roll(b_meta[pl.ds(c * 16 + 8, 8), :], 4, 0).astype(jnp.int32)
        b_slot = jnp.where(k8 < 4, b0, b1)
        live = (keep_ref[pl.ds(c * 8, 8), :] != 0) & (a_slot > 0) & (b_slot > 0)
        b_at = jnp.where(k8 < 4, 2 * c, 2 * c + 1) * SLOTS + b_slot - 1
        a_at = c * SLOTS + a_slot - 1
        table[pl.ds(c * 8, 8), :] = jnp.where(live, a_at + b_at * 65536, 0)
        bit = jnp.where(live, lax.shift_left(one, k8 + 8 * (c % 4)), 0)
        if c < 4:
            low = low | bit
        else:
            high = high | bit
    for n, word in enumerate((low, high)):
        word = word | pltpu.roll(word, 4, 0)
        word = word | pltpu.roll(word, 2, 0)
        word = word | pltpu.roll(word, 1, 0)
        words[pl.ds(8 * n, 8), :] = jnp.where(k8 == 0, word, lax.population_count(word))
    t0 = pltpu.make_async_copy(table, table_s, sem_t.at[0])
    t1 = pltpu.make_async_copy(words, words_s, sem_t.at[1])
    t0.start()
    t1.start()
    t0.wait()
    t1.wait()

    def block(p, _):
        acc = jnp.zeros((W, W), jnp.float32)
        for n in range(2):
            bits = words_s[8 * n, p]

            def step(_, state):
                bits, acc = state
                lowest = bits & -bits
                k = 31 - lax.clz(lowest) + 32 * n
                entry = table_s[k, p]
                a_at = pl.multiple_of((entry & 65535) * W, W)
                b_at = pl.multiple_of(lax.shift_right_logical(entry, 16) * W, W)
                a_high, a_low = split(a_all[pl.ds(a_at, W), :])
                b_high, b_low = split(b_all[pl.ds(b_at, W), :])
                left = jnp.concatenate([a_high, a_low], axis=1)
                right = jnp.concatenate(
                    [jnp.concatenate([b_high, b_low], axis=1), jnp.concatenate([b_low, b_high], axis=1)], axis=0
                )
                both = jnp.dot(left, right, preferred_element_type=jnp.float32)
                return bits ^ lowest, acc + (both[:, :W] + both[:, W:])

            bits, acc = lax.fori_loop(0, words_s[8 * n + 1, p], step, (bits, acc))
        i = p // 8
        j = p - i * 8
        out_ref[pl.ds(pl.multiple_of(i * W, W), W), pl.ds(pl.multiple_of(j * W, W), W)] = acc
        return 0

    lax.fori_loop(0, 32, block, 0)


def product(plan, where, keep_tile, pieces):
    hbm = pl.BlockSpec(memory_space=pl.ANY)
    return pl.pallas_call(
        functools.partial(product_kernel, plan),
        out_shape=jax.ShapeDtypeStruct((512, 1024), jnp.float32),
        in_specs=[pl.BlockSpec(memory_space=pltpu.SMEM), pl.BlockSpec(memory_space=pltpu.VMEM)] + [hbm] * len(pieces),
        out_specs=pl.BlockSpec(memory_space=pltpu.VMEM),
        scratch_shapes=[
            pltpu.VMEM((8 * DATA, W), jnp.float32),
            pltpu.VMEM((16 * DATA, W), jnp.float32),
            pltpu.VMEM((64, W), jnp.float32),
            pltpu.VMEM((128, W), jnp.float32),
            pltpu.VMEM((64, W), jnp.int32),
            pltpu.VMEM((16, W), jnp.int32),
            pltpu.SMEM((64, W), jnp.int32),
            pltpu.SMEM((16, W), jnp.int32),
            pltpu.SemaphoreType.DMA((2 * len(pieces),)),
            pltpu.SemaphoreType.DMA((2,)),
        ],
        compiler_params=pltpu.CompilerParams(vmem_limit_bytes=48 * 1024 * 1024),
        name="product",
    )(where, keep_tile, *pieces)


def swap(x, axis):
    return lax.ppermute(x, axis, [(0, 1), (1, 0)])


def right(x, axis):
    return lax.ppermute(x, axis, [(n, (n + 1) % 4) for n in range(4)])


def left(x, axis):
    return lax.ppermute(x, axis, [(n, (n - 1) % 4) for n in range(4)])


def ring(x, axis):
    from_left = right(x, axis)
    from_right = left(x, axis)
    first = right(from_left[:HALF], axis)
    second = left(from_right[HALF:], axis)
    return [(3, "whole", from_left), (1, "whole", from_right), (2, "first", first), (2, "second", second)]


def slots_of(mask):
    flat = (mask.reshape(-1) != 0).astype(jnp.float32)
    n = flat.shape[0]
    upto = jnp.asarray(np.tril(np.ones((n, n), np.float32)))
    rank = jnp.sum(upto * flat[None, :], axis=1)
    return (flat * rank).reshape(mask.shape)


def per_device(a_values, a_mask, b_values, b_mask, keep):
    a_slot = slots_of(a_mask)
    b_slot = slots_of(b_mask)
    a_tile = jnp.pad(jnp.repeat(a_slot.T, 8, axis=1), ((0, 0), (0, W - 32)))
    b_tile = jnp.pad(jnp.tile(b_slot, (1, 4)), ((0, 4), (0, W - 32)))
    keep_tile = jnp.pad(jnp.transpose(keep, (1, 0, 2)).reshape(64, 32), ((0, 0), (0, W - 32)))
    a, b = pack(a_mask, b_mask, a_values, b_values, a_tile, b_tile)

    zl, y, core = (lax.axis_index(n) for n in ROW)
    zh, x = (lax.axis_index(n) for n in COL)
    plan, where, pieces = [], [], []

    def add(which, part, at, piece):
        plan.append((which, part))
        where.append(at)
        pieces.append(piece)

    a_other = swap(a, "zh")
    b_other = swap(b, "zl")
    b_pieces = []
    for z, own_a, own_b in ((0, a, b), (1, a_other, b_other)):
        add("a", "whole", (zh ^ z) * 4 + x, own_a)
        for shift, part, piece in ring(own_a, "x"):
            add("a", part, (zh ^ z) * 4 + (x + shift) % 4, piece)
        b_pieces.append((z, 0, "whole", own_b))
        for shift, part, piece in ring(own_b, "y"):
            b_pieces.append((z, shift, part, piece))
    for z, shift, part, piece in b_pieces:
        chip = (zl ^ z) * 8 + ((y + shift) % 4) * 2
        add("b", part, chip + core, piece)
        add("b", part, chip + 1 - core, swap(piece, "core"))
    return product(tuple(plan), jnp.stack(where).astype(jnp.int32), keep_tile, pieces)


def solution(mesh):
    fine = Mesh(mesh.devices.reshape(2, 4, 2, 2, 4), ROW + COL)
    return jax.shard_map(
        per_device,
        mesh=fine,
        in_specs=(P(ROW, COL), P(ROW, COL), P(ROW, COL), P(ROW, COL), P(ROW, None, COL)),
        out_specs=P(ROW, COL),
        check_vma=False,
    )
```

```python
import functools

import jax
import jax.numpy as jnp
import numpy as np
from jax import lax
from jax.experimental import pallas as pl
from jax.experimental.pallas import tpu as pltpu
from jax.sharding import Mesh
from jax.sharding import PartitionSpec as P

W = 128
SLOTS = 20
DATA = SLOTS * W
ROWS = DATA + 8
HALF = DATA // 2
ROW = ("zl", "y", "core")
COL = ("zh", "x")


def pack_kernel(am_ref, bm_ref, a_ref, b_ref, am_tile, bm_tile, pa_ref, pb_ref, sem_a, sem_b, sem_m):
    tiles = (
        pltpu.make_async_copy(am_tile, pa_ref.at[pl.ds(DATA, 8), :], sem_m.at[0]),
        pltpu.make_async_copy(bm_tile, pb_ref.at[pl.ds(DATA, 8), :], sem_m.at[1]),
    )
    for tile in tiles:
        tile.start()

    def move(mask, src, dst, sem):
        rows, cols = mask.shape
        slot = jnp.int32(0)
        for r in range(rows):
            for c in range(cols):
                on = mask[r, c] != 0

                @pl.when(on)
                def _():
                    at = pl.multiple_of(slot * W, W)
                    pltpu.make_async_copy(
                        src.at[pl.ds(r * W, W), pl.ds(c * W, W)], dst.at[pl.ds(at, W), :], sem.at[r * cols + c]
                    ).start()

                slot = slot + on.astype(jnp.int32)

    def finish(mask, src, dst, sem):
        rows, cols = mask.shape
        for r in range(rows):
            for c in range(cols):

                @pl.when(mask[r, c] != 0)
                def _():
                    pltpu.make_async_copy(
                        src.at[pl.ds(r * W, W), pl.ds(c * W, W)], dst.at[pl.ds(0, W), :], sem.at[r * cols + c]
                    ).wait()

    move(am_ref, a_ref, pa_ref, sem_a)
    move(bm_ref, b_ref, pb_ref, sem_b)
    finish(am_ref, a_ref, pa_ref, sem_a)
    finish(bm_ref, b_ref, pb_ref, sem_b)
    for tile in tiles:
        tile.wait()


def pack(a_mask, b_mask, a_values, b_values, a_tile, b_tile):
    smem = pl.BlockSpec(memory_space=pltpu.SMEM)
    hbm = pl.BlockSpec(memory_space=pl.ANY)
    shape = jax.ShapeDtypeStruct((ROWS, W), jnp.float32)
    return pl.pallas_call(
        pack_kernel,
        out_shape=(shape, shape),
        in_specs=[smem, smem, hbm, hbm, hbm, hbm],
        out_specs=(pl.BlockSpec(memory_space=pltpu.VMEM), pl.BlockSpec(memory_space=pltpu.VMEM)),
        scratch_shapes=[
            pltpu.SemaphoreType.DMA((32,)),
            pltpu.SemaphoreType.DMA((32,)),
            pltpu.SemaphoreType.DMA((2,)),
        ],
        name="pack",
    )(a_mask, b_mask, a_values, b_values, a_tile, b_tile)


def split(x):
    high = x.astype(jnp.bfloat16)
    low = (x - high.astype(jnp.float32)).astype(jnp.bfloat16)
    return high, low


def product_kernel(plan, where_ref, keep_ref, *refs):
    count = len(plan)
    pieces = refs[:count]
    out_ref, a_all, b_all, a_meta, b_meta, table, words, table_s, words_s, sem, sem_t = refs[count:]
    copies = []
    for n, (which, part) in enumerate(plan):
        at = where_ref[n]
        data, meta, step = (a_all, a_meta, 8) if which == "a" else (b_all, b_meta, 8)
        base = at * DATA
        piece = pieces[n]
        if part != "first":
            copies.append((piece.at[pl.ds(piece.shape[0] - 8, 8), :], meta.at[pl.ds(at * 8, 8), :]))
        if part == "whole":
            copies.append((piece.at[pl.ds(0, DATA), :], data.at[pl.ds(base, DATA), :]))
        elif part == "first":
            copies.append((piece, data.at[pl.ds(base, HALF), :]))
        else:
            copies.append((piece.at[pl.ds(0, HALF), :], data.at[pl.ds(base + HALF, HALF), :]))
    copies = [pltpu.make_async_copy(src, dst, sem.at[n]) for n, (src, dst) in enumerate(copies)]
    for copy in copies:
        copy.start()
    for copy in copies:
        copy.wait()

    k8 = lax.broadcasted_iota(jnp.int32, (8, W), 0)
    one = jnp.ones((8, W), jnp.int32)
    low = jnp.zeros((8, W), jnp.int32)
    high = jnp.zeros((8, W), jnp.int32)
    for c in range(8):
        a_slot = a_meta[pl.ds(c * 8, 8), :].astype(jnp.int32)
        b0 = b_meta[pl.ds(c * 16, 8), :].astype(jnp.int32)
        b1 = pltpu.roll(b_meta[pl.ds(c * 16 + 8, 8), :], 4, 0).astype(jnp.int32)
        b_slot = jnp.where(k8 < 4, b0, b1)
        live = (keep_ref[pl.ds(c * 8, 8), :] != 0) & (a_slot > 0) & (b_slot > 0)
        b_at = jnp.where(k8 < 4, 2 * c, 2 * c + 1) * SLOTS + b_slot - 1
        a_at = c * SLOTS + a_slot - 1
        table[pl.ds(c * 8, 8), :] = jnp.where(live, a_at + b_at * 65536, 0)
        bit = jnp.where(live, lax.shift_left(one, k8 + 8 * (c % 4)), 0)
        if c < 4:
            low = low | bit
        else:
            high = high | bit
    for n, word in enumerate((low, high)):
        word = word | pltpu.roll(word, 4, 0)
        word = word | pltpu.roll(word, 2, 0)
        word = word | pltpu.roll(word, 1, 0)
        words[pl.ds(8 * n, 8), :] = jnp.where(k8 == 0, word, lax.population_count(word))
    t0 = pltpu.make_async_copy(table, table_s, sem_t.at[0])
    t1 = pltpu.make_async_copy(words, words_s, sem_t.at[1])
    t0.start()
    t1.start()
    t0.wait()
    t1.wait()

    def block(p, _):
        acc = jnp.zeros((W, W), jnp.float32)
        for n in range(2):
            bits = words_s[8 * n, p]

            def step(_, state):
                bits, acc = state
                lowest = bits & -bits
                k = 31 - lax.clz(lowest) + 32 * n
                entry = table_s[k, p]
                a_at = pl.multiple_of((entry & 65535) * W, W)
                b_at = pl.multiple_of(lax.shift_right_logical(entry, 16) * W, W)
                a_high, a_low = split(a_all[pl.ds(a_at, W), :])
                b_high, b_low = split(b_all[pl.ds(b_at, W), :])
                left = jnp.concatenate([a_high, a_low], axis=1)
                right = jnp.concatenate(
                    [jnp.concatenate([b_high, b_low], axis=1), jnp.concatenate([b_low, b_high], axis=1)], axis=0
                )
                both = jnp.dot(left, right, preferred_element_type=jnp.float32)
                return bits ^ lowest, acc + (both[:, :W] + both[:, W:])

            bits, acc = lax.fori_loop(0, words_s[8 * n + 1, p], step, (bits, acc))
        i = p // 8
        j = p - i * 8
        out_ref[pl.ds(pl.multiple_of(i * W, W), W), pl.ds(pl.multiple_of(j * W, W), W)] = acc
        return 0

    lax.fori_loop(0, 32, block, 0)


def product(plan, where, keep_tile, pieces):
    hbm = pl.BlockSpec(memory_space=pl.ANY)
    return pl.pallas_call(
        functools.partial(product_kernel, plan),
        out_shape=jax.ShapeDtypeStruct((512, 1024), jnp.float32),
        in_specs=[pl.BlockSpec(memory_space=pltpu.SMEM), pl.BlockSpec(memory_space=pltpu.VMEM)] + [hbm] * len(pieces),
        out_specs=pl.BlockSpec(memory_space=pltpu.VMEM),
        scratch_shapes=[
            pltpu.VMEM((8 * DATA, W), jnp.float32),
            pltpu.VMEM((16 * DATA, W), jnp.float32),
            pltpu.VMEM((64, W), jnp.float32),
            pltpu.VMEM((128, W), jnp.float32),
            pltpu.VMEM((64, W), jnp.int32),
            pltpu.VMEM((16, W), jnp.int32),
            pltpu.SMEM((64, W), jnp.int32),
            pltpu.SMEM((16, W), jnp.int32),
            pltpu.SemaphoreType.DMA((2 * len(pieces),)),
            pltpu.SemaphoreType.DMA((2,)),
        ],
        compiler_params=pltpu.CompilerParams(vmem_limit_bytes=48 * 1024 * 1024),
        name="product",
    )(where, keep_tile, *pieces)


def swap(x, axis):
    return lax.ppermute(x, axis, [(0, 1), (1, 0)])


def right(x, axis):
    return lax.ppermute(x, axis, [(n, (n + 1) % 4) for n in range(4)])


def left(x, axis):
    return lax.ppermute(x, axis, [(n, (n - 1) % 4) for n in range(4)])


def ring(x, axis, forward):
    from_left = right(x, axis)
    from_right = left(x, axis)
    far = right(from_left, axis) if forward else left(from_right, axis)
    return [(3, from_left), (1, from_right), (2, far)]


def slots_of(mask):
    flat = (mask.reshape(-1) != 0).astype(jnp.float32)
    n = flat.shape[0]
    upto = jnp.asarray(np.tril(np.ones((n, n), np.float32)))
    rank = jnp.sum(upto * flat[None, :], axis=1)
    return (flat * rank).reshape(mask.shape)


def per_device(a_values, a_mask, b_values, b_mask, keep):
    a_slot = slots_of(a_mask)
    b_slot = slots_of(b_mask)
    a_tile = jnp.pad(jnp.repeat(a_slot.T, 8, axis=1), ((0, 0), (0, W - 32)))
    b_tile = jnp.pad(jnp.tile(b_slot, (1, 4)), ((0, 4), (0, W - 32)))
    keep_tile = jnp.pad(jnp.transpose(keep, (1, 0, 2)).reshape(64, 32), ((0, 0), (0, W - 32)))
    a, b = pack(a_mask, b_mask, a_values, b_values, a_tile, b_tile)

    zl, y, core = (lax.axis_index(n) for n in ROW)
    zh, x = (lax.axis_index(n) for n in COL)
    plan, where, pieces = [], [], []

    def add(which, part, at, piece):
        plan.append((which, part))
        where.append(at)
        pieces.append(piece)

    a_other = swap(a, "zh")
    b_other = swap(b, "zl")
    b_pieces = []
    for z, own_a, own_b in ((0, a, b), (1, a_other, b_other)):
        add("a", "whole", (zh ^ z) * 4 + x, own_a)
        for shift, piece in ring(own_a, "x", z == 0):
            add("a", "whole", (zh ^ z) * 4 + (x + shift) % 4, piece)
        b_pieces.append((z, 0, own_b))
        for shift, piece in ring(own_b, "y", z == 0):
            b_pieces.append((z, shift, piece))
    for z, shift, piece in b_pieces:
        chip = (zl ^ z) * 8 + ((y + shift) % 4) * 2
        add("b", "whole", chip + core, piece)
        add("b", "whole", chip + 1 - core, swap(piece, "core"))
    return product(tuple(plan), jnp.stack(where).astype(jnp.int32), keep_tile, pieces)


def solution(mesh):
    fine = Mesh(mesh.devices.reshape(2, 4, 2, 2, 4), ROW + COL)
    return jax.shard_map(
        per_device,
        mesh=fine,
        in_specs=(P(ROW, COL), P(ROW, COL), P(ROW, COL), P(ROW, COL), P(ROW, None, COL)),
        out_specs=P(ROW, COL),
        check_vma=False,
    )
```

```python
import functools

import jax
import jax.numpy as jnp
import numpy as np
from jax import lax
from jax.experimental import pallas as pl
from jax.experimental.pallas import tpu as pltpu
from jax.sharding import Mesh
from jax.sharding import PartitionSpec as P

W = 128
SLOTS = 20
DATA = SLOTS * W
ROWS = DATA + 8
HALF = DATA // 2
ROW = ("zl", "y", "core")
COL = ("zh", "x")


def pack_kernel(am_ref, bm_ref, a_ref, b_ref, am_tile, bm_tile, pa_ref, pb_ref, sem_a, sem_b, sem_m):
    tiles = (
        pltpu.make_async_copy(am_tile, pa_ref.at[pl.ds(DATA, 8), :], sem_m.at[0]),
        pltpu.make_async_copy(bm_tile, pb_ref.at[pl.ds(DATA, 8), :], sem_m.at[1]),
    )
    for tile in tiles:
        tile.start()

    def move(mask, src, dst, sem):
        rows, cols = mask.shape
        slot = jnp.int32(0)
        for r in range(rows):
            for c in range(cols):
                on = mask[r, c] != 0

                @pl.when(on)
                def _():
                    at = pl.multiple_of(slot * W, W)
                    pltpu.make_async_copy(
                        src.at[pl.ds(r * W, W), pl.ds(c * W, W)], dst.at[pl.ds(at, W), :], sem.at[r * cols + c]
                    ).start()

                slot = slot + on.astype(jnp.int32)

    def finish(mask, src, dst, sem):
        rows, cols = mask.shape
        for r in range(rows):
            for c in range(cols):

                @pl.when(mask[r, c] != 0)
                def _():
                    pltpu.make_async_copy(
                        src.at[pl.ds(r * W, W), pl.ds(c * W, W)], dst.at[pl.ds(0, W), :], sem.at[r * cols + c]
                    ).wait()

    move(am_ref, a_ref, pa_ref, sem_a)
    move(bm_ref, b_ref, pb_ref, sem_b)
    finish(am_ref, a_ref, pa_ref, sem_a)
    finish(bm_ref, b_ref, pb_ref, sem_b)
    for tile in tiles:
        tile.wait()


def pack(a_mask, b_mask, a_values, b_values, a_tile, b_tile):
    smem = pl.BlockSpec(memory_space=pltpu.SMEM)
    hbm = pl.BlockSpec(memory_space=pl.ANY)
    shape = jax.ShapeDtypeStruct((ROWS, W), jnp.float32)
    return pl.pallas_call(
        pack_kernel,
        out_shape=(shape, shape),
        in_specs=[smem, smem, hbm, hbm, hbm, hbm],
        out_specs=(pl.BlockSpec(memory_space=pltpu.VMEM), pl.BlockSpec(memory_space=pltpu.VMEM)),
        scratch_shapes=[
            pltpu.SemaphoreType.DMA((32,)),
            pltpu.SemaphoreType.DMA((32,)),
            pltpu.SemaphoreType.DMA((2,)),
        ],
        name="pack",
    )(a_mask, b_mask, a_values, b_values, a_tile, b_tile)


def split(x):
    high = x.astype(jnp.bfloat16)
    low = (x - high.astype(jnp.float32)).astype(jnp.bfloat16)
    return high, low


def product_kernel(plan, where_ref, keep_ref, *refs):
    count = len(plan)
    pieces = refs[:count]
    out_ref, a_all, b_all, a_meta, b_meta, table, words, table_s, words_s, sem, sem_t = refs[count:]
    copies = []
    for n, (which, part) in enumerate(plan):
        at = where_ref[n]
        data, meta, step = (a_all, a_meta, 8) if which == "a" else (b_all, b_meta, 8)
        base = at * DATA
        piece = pieces[n]
        if part != "first":
            copies.append((piece.at[pl.ds(piece.shape[0] - 8, 8), :], meta.at[pl.ds(at * 8, 8), :]))
        if part == "whole":
            copies.append((piece.at[pl.ds(0, DATA), :], data.at[pl.ds(base, DATA), :]))
        elif part == "first":
            copies.append((piece, data.at[pl.ds(base, HALF), :]))
        else:
            copies.append((piece.at[pl.ds(0, HALF), :], data.at[pl.ds(base + HALF, HALF), :]))
    copies = [pltpu.make_async_copy(src, dst, sem.at[n]) for n, (src, dst) in enumerate(copies)]
    for copy in copies:
        copy.start()
    for copy in copies:
        copy.wait()

    k8 = lax.broadcasted_iota(jnp.int32, (8, W), 0)
    one = jnp.ones((8, W), jnp.int32)
    low = jnp.zeros((8, W), jnp.int32)
    high = jnp.zeros((8, W), jnp.int32)
    for c in range(8):
        a_slot = a_meta[pl.ds(c * 8, 8), :].astype(jnp.int32)
        b0 = b_meta[pl.ds(c * 16, 8), :].astype(jnp.int32)
        b1 = pltpu.roll(b_meta[pl.ds(c * 16 + 8, 8), :], 4, 0).astype(jnp.int32)
        b_slot = jnp.where(k8 < 4, b0, b1)
        live = (keep_ref[pl.ds(c * 8, 8), :] != 0) & (a_slot > 0) & (b_slot > 0)
        b_at = jnp.where(k8 < 4, 2 * c, 2 * c + 1) * SLOTS + b_slot - 1
        a_at = c * SLOTS + a_slot - 1
        table[pl.ds(c * 8, 8), :] = jnp.where(live, a_at + b_at * 65536, 0)
        bit = jnp.where(live, lax.shift_left(one, k8 + 8 * (c % 4)), 0)
        if c < 4:
            low = low | bit
        else:
            high = high | bit
    for n, word in enumerate((low, high)):
        word = word | pltpu.roll(word, 4, 0)
        word = word | pltpu.roll(word, 2, 0)
        word = word | pltpu.roll(word, 1, 0)
        words[pl.ds(8 * n, 8), :] = jnp.where(k8 == 0, word, lax.population_count(word))
    t0 = pltpu.make_async_copy(table, table_s, sem_t.at[0])
    t1 = pltpu.make_async_copy(words, words_s, sem_t.at[1])
    t0.start()
    t1.start()
    t0.wait()
    t1.wait()

    def block(p, _):
        acc = jnp.zeros((W, W), jnp.float32)
        for n in range(2):
            bits = words_s[8 * n, p]

            def step(_, state):
                bits, acc = state
                lowest = bits & -bits
                k = 31 - lax.clz(lowest) + 32 * n
                entry = table_s[k, p]
                a_at = pl.multiple_of((entry & 65535) * W, W)
                b_at = pl.multiple_of(lax.shift_right_logical(entry, 16) * W, W)
                a_high, a_low = split(a_all[pl.ds(a_at, W), :])
                b_high, b_low = split(b_all[pl.ds(b_at, W), :])
                left = jnp.concatenate([a_high, a_low], axis=1)
                right = jnp.concatenate(
                    [jnp.concatenate([b_high, b_low], axis=1), jnp.concatenate([b_low, b_high], axis=1)], axis=0
                )
                both = jnp.dot(left, right, preferred_element_type=jnp.float32)
                return bits ^ lowest, acc + (both[:, :W] + both[:, W:])

            bits, acc = lax.fori_loop(0, words_s[8 * n + 1, p], step, (bits, acc))
        i = p // 8
        j = p - i * 8
        out_ref[pl.ds(pl.multiple_of(i * W, W), W), pl.ds(pl.multiple_of(j * W, W), W)] = acc
        return 0

    lax.fori_loop(0, 32, block, 0)


def product(plan, where, keep_tile, pieces):
    hbm = pl.BlockSpec(memory_space=pl.ANY)
    return pl.pallas_call(
        functools.partial(product_kernel, plan),
        out_shape=jax.ShapeDtypeStruct((512, 1024), jnp.float32),
        in_specs=[pl.BlockSpec(memory_space=pltpu.SMEM), pl.BlockSpec(memory_space=pltpu.VMEM)] + [hbm] * len(pieces),
        out_specs=pl.BlockSpec(memory_space=pltpu.VMEM),
        scratch_shapes=[
            pltpu.VMEM((8 * DATA, W), jnp.float32),
            pltpu.VMEM((16 * DATA, W), jnp.float32),
            pltpu.VMEM((64, W), jnp.float32),
            pltpu.VMEM((128, W), jnp.float32),
            pltpu.VMEM((64, W), jnp.int32),
            pltpu.VMEM((16, W), jnp.int32),
            pltpu.SMEM((64, W), jnp.int32),
            pltpu.SMEM((16, W), jnp.int32),
            pltpu.SemaphoreType.DMA((2 * len(pieces),)),
            pltpu.SemaphoreType.DMA((2,)),
        ],
        compiler_params=pltpu.CompilerParams(vmem_limit_bytes=48 * 1024 * 1024),
        name="product",
    )(where, keep_tile, *pieces)


def swap(x, axis):
    return lax.ppermute(x, axis, [(0, 1), (1, 0)])


def right(x, axis):
    return lax.ppermute(x, axis, [(n, (n + 1) % 4) for n in range(4)])


def left(x, axis):
    return lax.ppermute(x, axis, [(n, (n - 1) % 4) for n in range(4)])


def opposite(from_left, from_right, core, axis):
    if axis == "x":
        axes, at = ("core", "x"), lambda n, c: c * 4 + n % 4
    else:
        axes, at = ("y", "core"), lambda n, c: n % 4 * 2 + c
    pairs = [(at(n, c), at(n + 1 - 2 * c, c)) for n in range(4) for c in range(2)]
    return lax.ppermute(jnp.where(core == 0, from_left, from_right), axes, pairs)


def after(x, *others):
    return lax.optimization_barrier((x, *others))[0]


def slots_of(mask):
    flat = (mask.reshape(-1) != 0).astype(jnp.float32)
    n = flat.shape[0]
    upto = jnp.asarray(np.tril(np.ones((n, n), np.float32)))
    rank = jnp.sum(upto * flat[None, :], axis=1)
    return (flat * rank).reshape(mask.shape)


def per_device(a_values, a_mask, b_values, b_mask, keep):
    a_slot = slots_of(a_mask)
    b_slot = slots_of(b_mask)
    a_tile = jnp.pad(jnp.repeat(a_slot.T, 8, axis=1), ((0, 0), (0, W - 32)))
    b_tile = jnp.pad(jnp.tile(b_slot, (1, 4)), ((0, 4), (0, W - 32)))
    keep_tile = jnp.pad(jnp.transpose(keep, (1, 0, 2)).reshape(64, 32), ((0, 0), (0, W - 32)))
    a, b = pack(a_mask, b_mask, a_values, b_values, a_tile, b_tile)

    zl, y, core = (lax.axis_index(n) for n in ROW)
    zh, x = (lax.axis_index(n) for n in COL)
    plan, where, pieces = [], [], []

    def add(which, part, at, piece):
        plan.append((which, part))
        where.append(at)
        pieces.append(piece)

    az = swap(a, "zh")
    ar, al = right(a, "x"), left(a, "x")
    br, bl = right(b, "y"), left(b, "y")
    phase = (az, ar, al, br, bl)
    ao = opposite(ar, al, core, "x")
    bo = opposite(br, bl, core, "y")
    bz = swap(after(b, *phase), "zl")
    azr, azl = right(after(az, *phase), "x"), left(after(az, *phase), "x")
    cb = swap(after(b, ao, bo), "core")
    cr = swap(after(br, ao, bo), "core")
    cl = swap(after(bl, cb, cr), "core")
    co = swap(after(bo, cb, cr), "core")
    phase = (bz, cl, co)
    bzr, bzl = right(after(bz, *phase), "y"), left(after(bz, *phase), "y")
    azo = opposite(after(azr, azl, *phase), after(azl, azr, *phase), core, "x")
    cz = swap(after(bz, *phase), "core")
    phase = (bzr, bzl, cz)
    bzo = opposite(after(bzr, *phase), after(bzl, *phase), core, "y")
    czr = swap(after(bzr, *phase), "core")
    czl = swap(after(bzl, *phase), "core")
    czo = swap(bzo, "core")
    for z, group in ((0, ((0, a), (3, ar), (1, al), (2, ao))), (1, ((0, az), (3, azr), (1, azl), (2, azo)))):
        for shift, piece in group:
            add("a", "whole", (zh ^ z) * 4 + (x + shift) % 4, piece)
    near = ((0, b, cb), (3, br, cr), (1, bl, cl), (2, bo, co))
    far = ((0, bz, cz), (3, bzr, czr), (1, bzl, czl), (2, bzo, czo))
    for z, group in ((0, near), (1, far)):
        for shift, mine, other in group:
            chip = (zl ^ z) * 8 + ((y + shift) % 4) * 2
            add("b", "whole", chip + core, mine)
            add("b", "whole", chip + 1 - core, other)
    return product(tuple(plan), jnp.stack(where).astype(jnp.int32), keep_tile, pieces)


def solution(mesh):
    fine = Mesh(mesh.devices.reshape(2, 4, 2, 2, 4), ROW + COL)
    return jax.shard_map(
        per_device,
        mesh=fine,
        in_specs=(P(ROW, COL), P(ROW, COL), P(ROW, COL), P(ROW, COL), P(ROW, None, COL)),
        out_specs=P(ROW, COL),
        check_vma=False,
    )
```

```python
import functools

import jax
import jax.numpy as jnp
import numpy as np
from jax import lax
from jax.experimental import pallas as pl
from jax.experimental.pallas import tpu as pltpu
from jax.sharding import Mesh
from jax.sharding import PartitionSpec as P

W = 128
SLOTS = 10
DATA = SLOTS * W
ROWS = DATA + 8
HALF = DATA // 2
ROW = ("zl", "y", "core")
COL = ("zh", "x")


def pack_kernel(am_ref, bm_ref, a_ref, b_ref, am_tile, bm_tile, pa_ref, pb_ref, qa_ref, qb_ref, sem_a, sem_b):
    pa_ref[pl.ds(DATA, 8), :] = am_tile[...]
    pb_ref[pl.ds(DATA, 8), :] = bm_tile[...]

    def copy(src, dst, sem, r, c, cols, at):
        return pltpu.make_async_copy(
            src.at[pl.ds(r * W, W), pl.ds(c * W, W)], dst.at[pl.ds(at, W), :], sem.at[r * cols + c]
        )

    def move(mask, src, main, rest, sem):
        rows, cols = mask.shape
        slot = jnp.int32(0)
        for r in range(rows):
            for c in range(cols):
                on = mask[r, c] != 0

                @pl.when(on & (slot < SLOTS))
                def _():
                    copy(src, main, sem, r, c, cols, pl.multiple_of(slot * W, W)).start()

                @pl.when(on & (slot >= SLOTS) & (slot < 2 * SLOTS))
                def _():
                    copy(src, rest, sem, r, c, cols, pl.multiple_of((slot - SLOTS) * W, W)).start()

                slot = slot + on.astype(jnp.int32)

    def finish(mask, src, main, sem):
        rows, cols = mask.shape
        for r in range(rows):
            for c in range(cols):

                @pl.when(mask[r, c] != 0)
                def _():
                    copy(src, main, sem, r, c, cols, 0).wait()

    move(am_ref, a_ref, pa_ref, qa_ref, sem_a)
    move(bm_ref, b_ref, pb_ref, qb_ref, sem_b)
    finish(am_ref, a_ref, pa_ref, sem_a)
    finish(bm_ref, b_ref, pb_ref, sem_b)


def pack(a_mask, b_mask, a_values, b_values, a_tile, b_tile):
    smem = pl.BlockSpec(memory_space=pltpu.SMEM)
    vmem = pl.BlockSpec(memory_space=pltpu.VMEM)
    hbm = pl.BlockSpec(memory_space=pl.ANY)
    main = jax.ShapeDtypeStruct((ROWS, W), jnp.float32)
    rest = jax.ShapeDtypeStruct((DATA, W), jnp.float32)
    return pl.pallas_call(
        pack_kernel,
        out_shape=(main, main, rest, rest),
        in_specs=[smem, smem, hbm, hbm, vmem, vmem],
        out_specs=(vmem,) * 4,
        scratch_shapes=[pltpu.SemaphoreType.DMA((32,)), pltpu.SemaphoreType.DMA((32,))],
        name="pack",
    )(a_mask, b_mask, a_values, b_values, a_tile, b_tile)


def split(x):
    high = x.astype(jnp.bfloat16)
    low = (x - high.astype(jnp.float32)).astype(jnp.bfloat16)
    return high, low


def product_kernel(plan, spread, where_ref, keep_ref, *refs):
    count = len(plan)
    pieces = refs[:count]
    out_ref, a_all, b_all, a_meta, b_meta, table, words, table_s, words_s, sem, sem_t = refs[count:]
    copies = []
    for n, (data, meta, first, rows) in enumerate(plan):
        at = where_ref[n]
        data = a_all if data == "a" else b_all
        copies.append((pieces[n].at[pl.ds(0, rows), :], data.at[pl.ds(first * W + at * rows, rows), :]))
        if meta:
            meta = a_meta if meta == "a" else b_meta
            copies.append((pieces[n].at[pl.ds(rows, 8), :], meta.at[pl.ds(at * 8, 8), :]))
    copies = [pltpu.make_async_copy(src, dst, sem.at[n]) for n, (src, dst) in enumerate(copies)]
    for copy in copies:
        copy.start()
    for copy in copies:
        copy.wait()

    def address(piece, rank, pieces):
        rest = pieces * SLOTS + rank - (SLOTS + 1)
        if spread:
            rest = rest + piece * SLOTS
        return jnp.where(rank <= SLOTS, piece * SLOTS + rank - 1, rest)

    k8 = lax.broadcasted_iota(jnp.int32, (8, W), 0)
    one = jnp.ones((8, W), jnp.int32)
    low = jnp.zeros((8, W), jnp.int32)
    high = jnp.zeros((8, W), jnp.int32)
    for c in range(8):
        a_slot = a_meta[pl.ds(c * 8, 8), :].astype(jnp.int32)
        b0 = b_meta[pl.ds(c * 16, 8), :].astype(jnp.int32)
        b1 = pltpu.roll(b_meta[pl.ds(c * 16 + 8, 8), :], 4, 0).astype(jnp.int32)
        b_slot = jnp.where(k8 < 4, b0, b1)
        live = (keep_ref[pl.ds(c * 8, 8), :] != 0) & (a_slot > 0) & (b_slot > 0)
        a_at = address(c, a_slot, 8)
        b_at = address(jnp.where(k8 < 4, 2 * c, 2 * c + 1), b_slot, 16)
        table[pl.ds(c * 8, 8), :] = jnp.where(live, a_at + b_at * 65536, 0)
        bit = jnp.where(live, lax.shift_left(one, k8 + 8 * (c % 4)), 0)
        if c < 4:
            low = low | bit
        else:
            high = high | bit
    for n, word in enumerate((low, high)):
        word = word | pltpu.roll(word, 4, 0)
        word = word | pltpu.roll(word, 2, 0)
        word = word | pltpu.roll(word, 1, 0)
        words[pl.ds(8 * n, 8), :] = jnp.where(k8 == 0, word, lax.population_count(word))
    t0 = pltpu.make_async_copy(table, table_s, sem_t.at[0])
    t1 = pltpu.make_async_copy(words, words_s, sem_t.at[1])
    t0.start()
    t1.start()
    t0.wait()
    t1.wait()

    def block(p, _):
        acc = jnp.zeros((W, W), jnp.float32)
        for n in range(2):
            bits = words_s[8 * n, p]

            def step(_, state):
                bits, acc = state
                lowest = bits & -bits
                k = 31 - lax.clz(lowest) + 32 * n
                entry = table_s[k, p]
                a_at = pl.multiple_of((entry & 65535) * W, W)
                b_at = pl.multiple_of(lax.shift_right_logical(entry, 16) * W, W)
                a_high, a_low = split(a_all[pl.ds(a_at, W), :])
                b_high, b_low = split(b_all[pl.ds(b_at, W), :])
                left = jnp.concatenate([a_high, a_low], axis=1)
                right = jnp.concatenate(
                    [jnp.concatenate([b_high, b_low], axis=1), jnp.concatenate([b_low, b_high], axis=1)], axis=0
                )
                both = jnp.dot(left, right, preferred_element_type=jnp.float32)
                return bits ^ lowest, acc + (both[:, :W] + both[:, W:])

            bits, acc = lax.fori_loop(0, words_s[8 * n + 1, p], step, (bits, acc))
        i = p // 8
        j = p - i * 8
        out_ref[pl.ds(pl.multiple_of(i * W, W), W), pl.ds(pl.multiple_of(j * W, W), W)] = acc
        return 0

    lax.fori_loop(0, 32, block, 0)


def product(spread, keep_tile, entries):
    hbm = pl.BlockSpec(memory_space=pl.ANY)
    plan = tuple(entry[:4] for entry in entries)
    where = jnp.stack([jnp.asarray(entry[4], jnp.int32) for entry in entries])
    pieces = [entry[5] for entry in entries]
    more = (8, 16) if spread else (1, 1)
    return pl.pallas_call(
        functools.partial(product_kernel, plan, spread),
        out_shape=jax.ShapeDtypeStruct((512, 1024), jnp.float32),
        in_specs=[pl.BlockSpec(memory_space=pltpu.SMEM), pl.BlockSpec(memory_space=pltpu.VMEM)] + [hbm] * len(pieces),
        out_specs=pl.BlockSpec(memory_space=pltpu.VMEM),
        scratch_shapes=[
            pltpu.VMEM(((8 + more[0]) * DATA, W), jnp.float32),
            pltpu.VMEM(((16 + more[1]) * DATA, W), jnp.float32),
            pltpu.VMEM((64, W), jnp.float32),
            pltpu.VMEM((128, W), jnp.float32),
            pltpu.VMEM((64, W), jnp.int32),
            pltpu.VMEM((16, W), jnp.int32),
            pltpu.SMEM((64, W), jnp.int32),
            pltpu.SMEM((16, W), jnp.int32),
            pltpu.SemaphoreType.DMA((2 * len(pieces),)),
            pltpu.SemaphoreType.DMA((2,)),
        ],
        compiler_params=pltpu.CompilerParams(vmem_limit_bytes=48 * 1024 * 1024),
        name="product",
    )(where, keep_tile, *pieces)


def swap(x, axis):
    return lax.ppermute(x, axis, [(0, 1), (1, 0)])


def right(x, axis):
    return lax.ppermute(x, axis, [(n, (n + 1) % 4) for n in range(4)])


def left(x, axis):
    return lax.ppermute(x, axis, [(n, (n - 1) % 4) for n in range(4)])


def opposite(from_left, from_right, core, axis):
    if axis == "x":
        axes, at = ("core", "x"), lambda n, c: c * 4 + n % 4
    else:
        axes, at = ("y", "core"), lambda n, c: n % 4 * 2 + c
    pairs = [(at(n, c), at(n + 1 - 2 * c, c)) for n in range(4) for c in range(2)]
    return lax.ppermute(jnp.where(core == 0, from_left, from_right), axes, pairs)


def gate(*done):
    return lambda x: lax.optimization_barrier((x, *done))[0]


def pair(x, axis, distance):
    return lax.ppermute(x, axis, [(n, n ^ distance) for n in range(4)])


def around(own, z, axis, core):
    other = swap(own, z)
    found = []
    for x in (own, other):
        r, l = right(x, axis), left(x, axis)
        found.append((x, r, l, opposite(r, l, core, axis)))
    return found


def slots_of(mask):
    flat = (mask.reshape(-1) != 0).astype(jnp.float32)
    n = flat.shape[0]
    upto = jnp.asarray(np.tril(np.ones((n, n), np.float32)))
    rank = jnp.sum(upto * flat[None, :], axis=1)
    return (flat * rank).reshape(mask.shape)


def per_device(a_values, a_mask, b_values, b_mask, keep):
    a_slot = slots_of(a_mask)
    b_slot = slots_of(b_mask)
    a_tile = jnp.pad(jnp.repeat(a_slot.T, 8, axis=1), ((0, 0), (0, W - 32)))
    b_tile = jnp.pad(jnp.tile(b_slot, (1, 4)), ((0, 4), (0, W - 32)))
    keep_tile = jnp.pad(jnp.transpose(keep, (1, 0, 2)).reshape(64, 32), ((0, 0), (0, W - 32)))
    a, b, a_rest, b_rest = pack(a_mask, b_mask, a_values, b_values, a_tile, b_tile)
    zl, y, core = (lax.axis_index(n) for n in ROW)
    zh, x = (lax.axis_index(n) for n in COL)

    az, ar, al, br, bl = swap(a, "zh"), right(a, "x"), left(a, "x"), right(b, "y"), left(b, "y")

    over = [(jnp.sum((m != 0).astype(jnp.int32)) > SLOTS).astype(jnp.float32) for m in (a_mask, b_mask)]
    flags = jnp.concatenate([jnp.full((4, W), n) for n in over])
    mine = [lax.dynamic_slice_in_dim(q, core * HALF, HALF) for q in (a_rest, b_rest)]
    theirs = [lax.dynamic_slice_in_dim(q, (1 - core) * HALF, HALF) for q in (a_rest, b_rest)]

    g = gate(az, ar, al, br, bl)
    bz, azr, azl = swap(g(b), "zl"), right(g(az), "x"), left(g(az), "x")
    bo = opposite(g(br), g(bl), core, "y")
    ec = swap(g(jnp.concatenate([*theirs, flags])), "core")
    cb = swap(gate(ec)(g(b)), "core")
    cr = swap(gate(cb)(g(br)), "core")
    cl = swap(gate(cr)(g(bl)), "core")

    excess = []
    for n in range(2):
        also = ec[2 * HALF + 4 * n, 0]
        piece = jnp.where(over[n] > 0, mine[n], jnp.where(also > 0, ec[n * HALF : (n + 1) * HALF], 0.0))
        excess.append(jnp.concatenate([piece, jnp.full((8, W), over[n] + also)]))
    ea, eb = excess

    g = gate(bz, azr, azl, bo, cl)
    bzr, bzl = right(g(bz), "y"), left(g(bz), "y")
    ao, azo = opposite(g(ar), g(al), core, "x"), opposite(g(azr), g(azl), core, "x")
    cz = swap(g(bz), "core")
    co = swap(gate(cz)(g(bo)), "core")
    eaz = swap(gate(cz)(g(ea)), "zh")
    ebz = swap(gate(co)(g(eb)), "zl")
    ea, eb = ea + eaz, eb + ebz

    g = gate(bzr, bzl, ao, azo, co, eaz, ebz)
    bzo = opposite(g(bzr), g(bzl), core, "y")
    czr = swap(g(bzr), "core")
    czl = swap(gate(czr)(g(bzl)), "core")
    eax, ebx = pair(g(ea), "x", 1), pair(g(eb), "y", 1)
    ea, eb = ea + eax, eb + ebx

    g = gate(bzo, czl, eax, ebx)
    czo = swap(g(bzo), "core")
    eax, ebx = pair(g(ea), "x", 2), pair(g(eb), "y", 2)
    ea, eb = ea + eax, eb + ebx
    last = swap(jnp.concatenate([ea[:HALF], eb[:HALF]]), "core")
    fa, fb = last[:HALF], last[HALF:]

    entries = []
    for z, group in ((0, (a, ar, al, ao)), (1, (az, azr, azl, azo))):
        for shift, piece in zip((0, 3, 1, 2), group):
            entries.append(("a", "a", 0, DATA, (zh ^ z) * 4 + (x + shift) % 4, piece))
    near = ((b, cb), (br, cr), (bl, cl), (bo, co))
    far = ((bz, cz), (bzr, czr), (bzl, czl), (bzo, czo))
    for z, group in ((0, near), (1, far)):
        for shift, both in zip((0, 3, 1, 2), group):
            chip = (zl ^ z) * 8 + ((y + shift) % 4) * 2
            entries.append(("b", "b", 0, DATA, chip + core, both[0]))
            entries.append(("b", "b", 0, DATA, chip + 1 - core, both[1]))
    crowded = [e[HALF, 0] > 1.5 for e in (ea, eb)]

    def few(_):
        more = [
            ("a", "", 8 * SLOTS, HALF, core, ea),
            ("a", "", 8 * SLOTS, HALF, 1 - core, fa),
            ("b", "", 16 * SLOTS, HALF, core, eb),
            ("b", "", 16 * SLOTS, HALF, 1 - core, fb),
        ]
        return product(False, keep_tile, entries + more)

    def many(_):
        def whole(e, f):
            e = e[:HALF]
            return jnp.where(core == 0, jnp.concatenate([e, f]), jnp.concatenate([f, e]))

        def all_a(_):
            near, far = around(a_rest, "zh", "x", core)
            return near + far

        def all_b(_):
            near, far = around(b_rest, "zl", "y", core)
            return near + far + tuple(swap(p, "core") for p in near + far)

        rest_a = lax.cond(crowded[0], all_a, lambda _: (whole(ea, fa),) * 8, 0)
        rest_b = lax.cond(crowded[1], all_b, lambda _: (whole(eb, fb),) * 16, 0)
        more = []
        for n, piece in enumerate(rest_a):
            more.append(("a", "", 8 * SLOTS, DATA, (zh ^ (n // 4)) * 4 + (x + (0, 3, 1, 2)[n % 4]) % 4, piece))
        for n, piece in enumerate(rest_b):
            chip = (zl ^ (n // 4 % 2)) * 8 + ((y + (0, 3, 1, 2)[n % 4]) % 4) * 2
            more.append(("b", "", 16 * SLOTS, DATA, chip + (core if n < 8 else 1 - core), piece))
        return product(True, keep_tile, entries + more)

    return lax.cond(crowded[0] | crowded[1], many, few, 0)


def solution(mesh):
    fine = Mesh(mesh.devices.reshape(2, 4, 2, 2, 4), ROW + COL)
    return jax.shard_map(
        per_device,
        mesh=fine,
        in_specs=(P(ROW, COL), P(ROW, COL), P(ROW, COL), P(ROW, COL), P(ROW, None, COL)),
        out_specs=P(ROW, COL),
        check_vma=False,
    )
```

```python
import functools

import jax
import jax.numpy as jnp
from jax import lax
from jax.experimental import pallas as pl
from jax.experimental.pallas import tpu as pltpu
from jax.sharding import Mesh
from jax.sharding import PartitionSpec as P

W = 128
SLOTS = 10
DATA = SLOTS * W
ROWS = DATA + 8
HALF = DATA // 2
ROW = ("zl", "y", "core")
COL = ("zh", "x")


def pack_kernel(core_ref, am_ref, bm_ref, a_ref, b_ref, pa_ref, pb_ref, mine_ref, theirs_ref, sem_a, sem_b):
    core = core_ref[0]
    row = lax.broadcasted_iota(jnp.int32, (8, W), 0)
    lane = lax.broadcasted_iota(jnp.int32, (8, W), 1)

    def copy(src, dst, sem, r, c, cols, at):
        return pltpu.make_async_copy(
            src.at[pl.ds(r * W, W), pl.ds(c * W, W)], dst.at[pl.ds(at, W), :], sem.at[r * cols + c]
        )

    def move(mask, src, main, base, sem, spot):
        rows, cols = mask.shape
        slot = jnp.int32(0)
        tile = jnp.zeros((8, W), jnp.float32)
        for r in range(rows):
            for c in range(cols):
                on = mask[r, c] != 0
                rest = slot - SLOTS
                second = rest >= SLOTS // 2
                inside = (rest >= 0) & (rest < SLOTS)
                half = second.astype(jnp.int32)
                at = base + (rest - half * (SLOTS // 2)) * W

                @pl.when(on & (rest < 0))
                def _():
                    copy(src, main, sem, r, c, cols, pl.multiple_of(slot * W, W)).start()

                @pl.when(on & inside & (half == core))
                def _():
                    copy(src, mine_ref, sem, r, c, cols, pl.multiple_of(at, W)).start()

                @pl.when(on & inside & (half != core))
                def _():
                    copy(src, theirs_ref, sem, r, c, cols, pl.multiple_of(at, W)).start()

                slot = slot + on.astype(jnp.int32)
                tile = jnp.where(spot(r, c), jnp.where(on, slot, 0).astype(jnp.float32), tile)
        main[pl.ds(DATA, 8), :] = tile
        return slot > SLOTS

    def finish(mask, src, main, sem):
        rows, cols = mask.shape
        for r in range(rows):
            for c in range(cols):

                @pl.when(mask[r, c] != 0)
                def _():
                    copy(src, main, sem, r, c, cols, 0).wait()

    over_a = move(am_ref, a_ref, pa_ref, 0, sem_a, lambda r, c: (row == c) & (lane // 8 == r))
    over_b = move(bm_ref, b_ref, pb_ref, HALF, sem_b, lambda r, c: (row == r) & (lane % 8 == c))
    flags = jnp.where(row < 4, over_a.astype(jnp.float32), over_b.astype(jnp.float32))
    mine_ref[pl.ds(DATA, 8), :] = flags
    theirs_ref[pl.ds(DATA, 8), :] = flags
    finish(am_ref, a_ref, pa_ref, sem_a)
    finish(bm_ref, b_ref, pb_ref, sem_b)


def pack(core, a_mask, b_mask, a_values, b_values):
    smem = pl.BlockSpec(memory_space=pltpu.SMEM)
    vmem = pl.BlockSpec(memory_space=pltpu.VMEM)
    hbm = pl.BlockSpec(memory_space=pl.ANY)
    return pl.pallas_call(
        pack_kernel,
        out_shape=(jax.ShapeDtypeStruct((ROWS, W), jnp.float32),) * 4,
        in_specs=[smem, smem, smem, hbm, hbm],
        out_specs=(vmem,) * 4,
        scratch_shapes=[pltpu.SemaphoreType.DMA((32,)), pltpu.SemaphoreType.DMA((32,))],
        name="pack",
    )(core.reshape(1).astype(jnp.int32), a_mask, b_mask, a_values, b_values)


def merge_kernel(mine_ref, theirs_ref, a_ref, b_ref):
    for n, out_ref in enumerate((a_ref, b_ref)):
        own = mine_ref[pl.ds(DATA + 4 * n, 1), :]
        also = theirs_ref[pl.ds(DATA + 4 * n, 1), :]
        kept = jnp.where(also > 0, theirs_ref[pl.ds(n * HALF, HALF), :], 0.0)
        out_ref[pl.ds(0, HALF), :] = jnp.where(own > 0, mine_ref[pl.ds(n * HALF, HALF), :], kept)
        out_ref[pl.ds(HALF, 8), :] = jnp.broadcast_to(own + also, (8, W))


def merge(mine, theirs):
    vmem = pl.BlockSpec(memory_space=pltpu.VMEM)
    return pl.pallas_call(
        merge_kernel,
        out_shape=(jax.ShapeDtypeStruct((HALF + 8, W), jnp.float32),) * 2,
        in_specs=[vmem, vmem],
        out_specs=(vmem, vmem),
        name="merge",
    )(mine, theirs)


def split(x):
    high = x.astype(jnp.bfloat16)
    low = (x - high.astype(jnp.float32)).astype(jnp.bfloat16)
    return high, low


def product_kernel(plan, spread, where_ref, keep_ref, *refs):
    count = len(plan)
    pieces = refs[:count]
    out_ref, acc, a_all, b_all, a_meta, b_meta, table, words, table_s, words_s, list_s, sem, sem_t, sem_o = refs[count:]
    copies = []
    for n, (data, meta, first, rows) in enumerate(plan):
        at = where_ref[n]
        data = a_all if data == "a" else b_all
        copies.append((pieces[n].at[pl.ds(0, rows), :], data.at[pl.ds(first * W + at * rows, rows), :]))
        if meta:
            meta = a_meta if meta == "a" else b_meta
            copies.append((pieces[n].at[pl.ds(rows, 8), :], meta.at[pl.ds(at * 8, 8), :]))
    copies = [pltpu.make_async_copy(src, dst, sem.at[n]) for n, (src, dst) in enumerate(copies)]
    for copy in copies:
        copy.start()
    acc[...] = jnp.zeros(acc.shape, jnp.float32)
    for copy in copies:
        copy.wait()

    def address(piece, rank, pieces):
        rest = pieces * SLOTS + rank - (SLOTS + 1)
        if spread:
            rest = rest + piece * SLOTS
        return jnp.where(rank <= SLOTS, piece * SLOTS + rank - 1, rest)

    k8 = lax.broadcasted_iota(jnp.int32, (8, W), 0)
    one = jnp.ones((8, W), jnp.int32)
    low = jnp.zeros((8, W), jnp.int32)
    high = jnp.zeros((8, W), jnp.int32)
    for c in range(8):
        a_slot = a_meta[pl.ds(c * 8, 8), :].astype(jnp.int32)
        b0 = b_meta[pl.ds(c * 16, 8), :].astype(jnp.int32)
        b1 = pltpu.roll(b_meta[pl.ds(c * 16 + 8, 8), :], 4, 0).astype(jnp.int32)
        b_slot = jnp.where(k8 < 4, b0, b1)
        live = (keep_ref[pl.ds(c * 8, 8), :] != 0) & (a_slot > 0) & (b_slot > 0)
        a_at = address(c, a_slot, 8)
        b_at = address(jnp.where(k8 < 4, 2 * c, 2 * c + 1), b_slot, 16)
        table[pl.ds(c * 8, 8), :] = jnp.where(live, a_at + b_at * 65536, 0)
        bit = jnp.where(live, lax.shift_left(one, k8 + 8 * (c % 4)), 0)
        if c < 4:
            low = low | bit
        else:
            high = high | bit
    for n, word in enumerate((low, high)):
        word = word | pltpu.roll(word, 4, 0)
        word = word | pltpu.roll(word, 2, 0)
        word = word | pltpu.roll(word, 1, 0)
        words[pl.ds(8 * n, 8), :] = jnp.where(k8 == 0, word, lax.population_count(word))
    t0 = pltpu.make_async_copy(table, table_s, sem_t.at[0])
    t1 = pltpu.make_async_copy(words, words_s, sem_t.at[1])
    t0.start()
    t1.start()
    t0.wait()
    t1.wait()

    def gather(p, total):
        for n in range(2):

            def one(m, bits):
                lowest = bits & -bits
                k = 31 - lax.clz(lowest) + 32 * n
                list_s[0, total + m] = table_s[k, p]
                list_s[1, total + m] = p
                return bits ^ lowest

            found = words_s[8 * n + 1, p]
            lax.fori_loop(0, found, one, words_s[8 * n, p])
            total = total + found
        return total

    def term(entry):
        a_at = pl.multiple_of((entry & 65535) * W, W)
        b_at = pl.multiple_of(lax.shift_right_logical(entry, 16) * W, W)
        a_high, a_low = split(a_all[pl.ds(a_at, W), :])
        b_high, b_low = split(b_all[pl.ds(b_at, W), :])
        left = jnp.concatenate([a_high, a_low], axis=1)
        right = jnp.concatenate(
            [jnp.concatenate([b_high, b_low], axis=1), jnp.concatenate([b_low, b_high], axis=1)], axis=0
        )
        both = jnp.dot(left, right, preferred_element_type=jnp.float32)
        return both[:, :W] + both[:, W:]

    def place(p):
        return pl.ds(pl.multiple_of(p // 8 * W, W), W), pl.ds(pl.multiple_of(p % 8 * W, W), W)

    total = lax.fori_loop(0, 32, gather, jnp.int32(0))

    def four(t, _):
        terms = [term(list_s[0, 4 * t + n]) for n in range(4)]
        for n in range(4):
            rows, cols = place(list_s[1, 4 * t + n])
            acc[rows, cols] = acc[rows, cols] + terms[n]
        return 0

    def single(t, _):
        rows, cols = place(list_s[1, t])
        acc[rows, cols] = acc[rows, cols] + term(list_s[0, t])
        return 0

    lax.fori_loop(0, total // 4, four, 0)
    lax.fori_loop(total // 4 * 4, total, single, 0)
    out = pltpu.make_async_copy(acc, out_ref, sem_o)
    out.start()
    out.wait()


def product(spread, keep_tile, entries):
    hbm = pl.BlockSpec(memory_space=pl.ANY)
    plan = tuple(entry[:4] for entry in entries)
    where = jnp.stack([jnp.asarray(entry[4], jnp.int32) for entry in entries])
    pieces = [entry[5] for entry in entries]
    more = (8, 16) if spread else (1, 1)
    return pl.pallas_call(
        functools.partial(product_kernel, plan, spread),
        out_shape=jax.ShapeDtypeStruct((512, 1024), jnp.float32),
        in_specs=[pl.BlockSpec(memory_space=pltpu.SMEM), pl.BlockSpec(memory_space=pltpu.VMEM)] + [hbm] * len(pieces),
        out_specs=hbm,
        scratch_shapes=[
            pltpu.VMEM((512, 1024), jnp.float32),
            pltpu.VMEM(((8 + more[0]) * DATA, W), jnp.float32),
            pltpu.VMEM(((16 + more[1]) * DATA, W), jnp.float32),
            pltpu.VMEM((64, W), jnp.float32),
            pltpu.VMEM((128, W), jnp.float32),
            pltpu.VMEM((64, W), jnp.int32),
            pltpu.VMEM((16, W), jnp.int32),
            pltpu.SMEM((64, W), jnp.int32),
            pltpu.SMEM((16, W), jnp.int32),
            pltpu.SMEM((2, 2048), jnp.int32),
            pltpu.SemaphoreType.DMA((2 * len(pieces),)),
            pltpu.SemaphoreType.DMA((2,)),
            pltpu.SemaphoreType.DMA,
        ],
        compiler_params=pltpu.CompilerParams(vmem_limit_bytes=48 * 1024 * 1024),
        name="product",
    )(where, keep_tile, *pieces)


def swap(x, axis):
    return lax.ppermute(x, axis, [(0, 1), (1, 0)])


def right(x, axis):
    return lax.ppermute(x, axis, [(n, (n + 1) % 4) for n in range(4)])


def left(x, axis):
    return lax.ppermute(x, axis, [(n, (n - 1) % 4) for n in range(4)])


def opposite(from_left, from_right, core, axis):
    if axis == "x":
        axes, at = ("core", "x"), lambda n, c: c * 4 + n % 4
    else:
        axes, at = ("y", "core"), lambda n, c: n % 4 * 2 + c
    pairs = [(at(n, c), at(n + 1 - 2 * c, c)) for n in range(4) for c in range(2)]
    return lax.ppermute(jnp.where(core == 0, from_left, from_right), axes, pairs)


def gate(*done):
    return lambda x: lax.optimization_barrier((x, *done))[0]


def pair(x, axis, distance):
    return lax.ppermute(x, axis, [(n, n ^ distance) for n in range(4)])


def around(own, z, axis, core):
    other = swap(own, z)
    found = []
    for x in (own, other):
        r, l = right(x, axis), left(x, axis)
        found.append((x, r, l, opposite(r, l, core, axis)))
    return found


def per_device(a_values, a_mask, b_values, b_mask, keep):
    zl, y, core = (lax.axis_index(n) for n in ROW)
    zh, x = (lax.axis_index(n) for n in COL)
    keep_tile = jnp.pad(jnp.transpose(keep, (1, 0, 2)).reshape(64, 32), ((0, 0), (0, W - 32)))
    a, b, mine, theirs = pack(core, a_mask, b_mask, a_values, b_values)

    ar, al, br, bl = right(a, "x"), left(a, "x"), right(b, "y"), left(b, "y")
    az = swap(a, "zh")
    ea, eb = merge(mine, swap(theirs, "core"))
    eaz, ebz = swap(ea, "zh"), swap(eb, "zl")

    ga, gb = gate(az, ar, al, eaz), gate(az, br, bl, ebz)
    azr, azl = right(ga(az), "x"), left(ga(az), "x")
    bz = swap(gb(b), "zl")
    bo = opposite(gb(br), gb(bl), core, "y")
    ea, eb = ea + eaz, eb + ebz
    eax, ebx = pair(ga(ea), "x", 1), pair(gb(eb), "y", 1)
    cb = swap(gb(b), "core")
    cr = swap(gate(cb)(gb(br)), "core")
    cl = swap(gate(cr)(gb(bl)), "core")

    ga, gb = gate(azr, azl, eax), gate(bz, bo, cl, ebx)
    bzr, bzl = right(gb(bz), "y"), left(gb(bz), "y")
    ao, azo = opposite(ga(ar), ga(al), core, "x"), opposite(ga(azr), ga(azl), core, "x")
    ea, eb = ea + eax, eb + ebx
    eax, ebx = pair(ga(ea), "x", 2), pair(gb(eb), "y", 2)
    cz = swap(gb(bz), "core")
    co = swap(gate(cz)(gb(bo)), "core")

    ea, eb = ea + eax, eb + ebx
    gb = gate(bzr, bzl, co, ao, azo, eax, ebx)
    bzo = opposite(gb(bzr), gb(bzl), core, "y")
    czr = swap(gb(bzr), "core")
    fa, fb = swap(gb(ea), "core"), swap(gate(czr)(gb(eb)), "core")
    czl = swap(gate(fb)(gb(bzl)), "core")
    czo = swap(bzo, "core")

    entries = []
    for z, group in ((0, (a, ar, al, ao)), (1, (az, azr, azl, azo))):
        for shift, piece in zip((0, 3, 1, 2), group):
            entries.append(("a", "a", 0, DATA, (zh ^ z) * 4 + (x + shift) % 4, piece))
    near = ((b, cb), (br, cr), (bl, cl), (bo, co))
    far = ((bz, cz), (bzr, czr), (bzl, czl), (bzo, czo))
    for z, group in ((0, near), (1, far)):
        for shift, both in zip((0, 3, 1, 2), group):
            chip = (zl ^ z) * 8 + ((y + shift) % 4) * 2
            entries.append(("b", "b", 0, DATA, chip + core, both[0]))
            entries.append(("b", "b", 0, DATA, chip + 1 - core, both[1]))
    crowded = [e[HALF, 0] > 1.5 for e in (ea, eb)]

    def few(_):
        more = [
            ("a", "", 8 * SLOTS, HALF, core, ea),
            ("a", "", 8 * SLOTS, HALF, 1 - core, fa),
            ("b", "", 16 * SLOTS, HALF, core, eb),
            ("b", "", 16 * SLOTS, HALF, 1 - core, fb),
        ]
        return product(False, keep_tile, entries + more)

    def many(_):
        def whole(e, f):
            e, f = e[:HALF], f[:HALF]
            return jnp.where(core == 0, jnp.concatenate([e, f]), jnp.concatenate([f, e]))

        def all_a(_):
            near, far = around(rest(0), "zh", "x", core)
            return near + far

        def all_b(_):
            near, far = around(rest(1), "zl", "y", core)
            return near + far + tuple(swap(p, "core") for p in near + far)

        def rest(n):
            parts = [q[n * HALF : (n + 1) * HALF] for q in (mine, theirs)]
            return jnp.where(core == 0, jnp.concatenate(parts), jnp.concatenate(parts[::-1]))

        rest_a = lax.cond(crowded[0], all_a, lambda _: (whole(ea, fa),) * 8, 0)
        rest_b = lax.cond(crowded[1], all_b, lambda _: (whole(eb, fb),) * 16, 0)
        more = []
        for n, piece in enumerate(rest_a):
            more.append(("a", "", 8 * SLOTS, DATA, (zh ^ (n // 4)) * 4 + (x + (0, 3, 1, 2)[n % 4]) % 4, piece))
        for n, piece in enumerate(rest_b):
            chip = (zl ^ (n // 4 % 2)) * 8 + ((y + (0, 3, 1, 2)[n % 4]) % 4) * 2
            more.append(("b", "", 16 * SLOTS, DATA, chip + (core if n < 8 else 1 - core), piece))
        return product(True, keep_tile, entries + more)

    return lax.cond(crowded[0] | crowded[1], many, few, 0)


def solution(mesh):
    fine = Mesh(mesh.devices.reshape(2, 4, 2, 2, 4), ROW + COL)
    return jax.shard_map(
        per_device,
        mesh=fine,
        in_specs=(P(ROW, COL), P(ROW, COL), P(ROW, COL), P(ROW, COL), P(ROW, None, COL)),
        out_specs=P(ROW, COL),
        check_vma=False,
    )
```

```python
import functools

import jax
import jax.numpy as jnp
import numpy as np
from jax import lax
from jax.experimental import pallas as pl
from jax.experimental.pallas import tpu as pltpu
from jax.sharding import Mesh
from jax.sharding import PartitionSpec as P

W = 128
SLOTS = 10
DATA = SLOTS * W
TILES = 2 * DATA
ROWS = TILES + 16
ROW = ("zl", "y", "core")
COL = ("zh", "x")


def pack_kernel(core_ref, am_ref, bm_ref, a_ref, b_ref, keep_ref, send_ref, sem):
    core = core_ref[0]
    row = lax.broadcasted_iota(jnp.int32, (8, W), 0)
    lane = lax.broadcasted_iota(jnp.int32, (8, W), 1)
    factors = (
        (am_ref, a_ref, lambda r, c: (row == c) & (lane // 8 == r)),
        (bm_ref, b_ref, lambda r, c: (row == r) & (lane % 8 == c)),
    )

    def copy(n, src, dst, r, c, cols, at):
        return pltpu.make_async_copy(
            src.at[pl.ds(r * W, W), pl.ds(c * W, W)], dst.at[pl.ds(at, W), :], sem.at[n * 32 + r * cols + c]
        )

    for n, (mask, src, spot) in enumerate(factors):
        rows, cols = mask.shape
        slot = jnp.int32(0)
        tile = jnp.zeros((8, W), jnp.float32)
        for r in range(rows):
            for c in range(cols):
                on = mask[r, c] != 0
                fits = on & (slot < 2 * SLOTS)
                at = pl.multiple_of(slot * W, W)
                for dst, here in ((keep_ref, core == n), (send_ref, core != n)):

                    @pl.when(fits & here)
                    def _():
                        copy(n, src, dst, r, c, cols, at).start()

                slot = slot + on.astype(jnp.int32)
                tile = jnp.where(spot(r, c), jnp.where(on, slot, 0).astype(jnp.float32), tile)
        flag = jnp.zeros((8, W), jnp.float32) + jnp.where(slot > SLOTS, 1.0, 0.0)
        for dst, here in ((keep_ref, core == n), (send_ref, core != n)):

            @pl.when(here)
            def _():
                dst[pl.ds(TILES, 8), :] = tile
                dst[pl.ds(TILES + 8, 8), :] = flag

    for n, (mask, src, _) in enumerate(factors):
        rows, cols = mask.shape
        for r in range(rows):
            for c in range(cols):

                @pl.when(mask[r, c] != 0)
                def _():
                    copy(n, src, keep_ref, r, c, cols, 0).wait()


def pack(core, a_mask, b_mask, a_values, b_values):
    smem = pl.BlockSpec(memory_space=pltpu.SMEM)
    vmem = pl.BlockSpec(memory_space=pltpu.VMEM)
    hbm = pl.BlockSpec(memory_space=pl.ANY)
    return pl.pallas_call(
        pack_kernel,
        out_shape=(jax.ShapeDtypeStruct((ROWS, W), jnp.float32),) * 2,
        in_specs=[smem, smem, smem, hbm, hbm],
        out_specs=(vmem,) * 2,
        scratch_shapes=[pltpu.SemaphoreType.DMA((64,))],
        name="pack",
    )(core, a_mask, b_mask, a_values, b_values)


def merge_kernel(core_ref, keep_ref, got_ref, main_ref, excess_ref):
    core = core_ref[0]
    for ref, at in ((keep_ref, core), (got_ref, 1 - core)):
        main_ref[pl.ds(pl.multiple_of(at * DATA, DATA), DATA), :] = ref[pl.ds(0, DATA), :]
        main_ref[pl.ds(pl.multiple_of(TILES + at * 8, 8), 8), :] = ref[pl.ds(TILES, 8), :]
    own = keep_ref[pl.ds(TILES + 8, 8), :]
    also = got_ref[pl.ds(TILES + 8, 8), :]
    kept = jnp.where(also[:1] > 0, got_ref[pl.ds(DATA, DATA), :], 0.0)
    excess_ref[pl.ds(0, DATA), :] = jnp.where(own[:1] > 0, keep_ref[pl.ds(DATA, DATA), :], kept)
    excess_ref[pl.ds(DATA, 8), :] = own + also


def merge(core, keep, got):
    vmem = pl.BlockSpec(memory_space=pltpu.VMEM)
    return pl.pallas_call(
        merge_kernel,
        out_shape=(
            jax.ShapeDtypeStruct((ROWS, W), jnp.float32),
            jax.ShapeDtypeStruct((DATA + 8, W), jnp.float32),
        ),
        in_specs=[pl.BlockSpec(memory_space=pltpu.SMEM), vmem, vmem],
        out_specs=(vmem, vmem),
        name="merge",
    )(core, keep, got)


def split(x):
    high = x.astype(jnp.bfloat16)
    low = (x - high.astype(jnp.float32)).astype(jnp.bfloat16)
    return high, low


def product_kernel(shapes, spread, where_ref, keep_ref, *refs):
    count = sum(shapes)
    pieces = list(refs[:count])
    out_ref, acc, a_all, b_all, a_meta, b_meta, table, words, table_s, words_s, list_s, sem, sem_t, sem_o = refs[count:]
    core = where_ref[0]
    groups = []
    for size in shapes:
        groups.append(pieces[:size])
        pieces = pieces[size:]
    lines, extra = groups[:17], groups[17:]

    def parts(piece):
        if len(piece) == 1:
            return [piece[0].at[pl.ds(0, DATA), :], piece[0].at[pl.ds(DATA, DATA), :], piece[0].at[pl.ds(TILES, 16), :]]
        return [piece[0], piece[1].at[pl.ds(0, DATA), :], piece[1].at[pl.ds(DATA, 16), :]]

    def copies(side):
        found = []
        for n in range(8):
            a_at, b_at = where_ref[1 + n], where_ref[9 + n]
            pair = (parts(lines[2 * n]), parts(lines[2 * n + 1]))
            a_parts, b_parts = pair[side], pair[1 - side]
            found.append((a_parts[side], a_all.at[pl.ds(a_at * DATA, DATA), :]))
            found.append((a_parts[2].at[pl.ds(8 * side, 8), :], a_meta.at[pl.ds(a_at * 8, 8), :]))
            for h in range(2):
                found.append((b_parts[h], b_all.at[pl.ds((b_at * 2 + h) * DATA, DATA), :]))
            found.append((b_parts[2], b_meta.at[pl.ds(b_at * 16, 16), :]))
        if not spread:
            e = lines[16]
            found.append((e[side].at[pl.ds(0, DATA), :], a_all.at[pl.ds(8 * DATA, DATA), :]))
            found.append((e[1 - side].at[pl.ds(0, DATA), :], b_all.at[pl.ds(16 * DATA, DATA), :]))
        for n, piece in enumerate(extra):
            if n < 8:
                found.append((piece[0], a_all.at[pl.ds((8 + where_ref[1 + n]) * DATA, DATA), :]))
            else:
                h = side if n < 16 else 1 - side
                at = 16 + where_ref[9 + n % 8] * 2 + h
                found.append((piece[0], b_all.at[pl.ds(at * DATA, DATA), :]))
        return [pltpu.make_async_copy(src, dst, sem.at[n]) for n, (src, dst) in enumerate(found)]

    for side in range(2):

        @pl.when(core == side)
        def _():
            for copy in copies(side):
                copy.start()

    acc[...] = jnp.zeros(acc.shape, jnp.float32)
    for side in range(2):

        @pl.when(core == side)
        def _():
            for copy in copies(side):
                copy.wait()

    def address(piece, rank, pieces):
        rest = pieces * SLOTS + rank - (SLOTS + 1)
        if spread:
            rest = rest + piece * SLOTS
        return jnp.where(rank <= SLOTS, piece * SLOTS + rank - 1, rest)

    k8 = lax.broadcasted_iota(jnp.int32, (8, W), 0)
    one = jnp.ones((8, W), jnp.int32)
    low = jnp.zeros((8, W), jnp.int32)
    high = jnp.zeros((8, W), jnp.int32)
    for c in range(8):
        a_slot = a_meta[pl.ds(c * 8, 8), :].astype(jnp.int32)
        b0 = b_meta[pl.ds(c * 16, 8), :].astype(jnp.int32)
        b1 = pltpu.roll(b_meta[pl.ds(c * 16 + 8, 8), :], 4, 0).astype(jnp.int32)
        b_slot = jnp.where(k8 < 4, b0, b1)
        live = (keep_ref[pl.ds(c * 8, 8), :] != 0) & (a_slot > 0) & (b_slot > 0)
        a_at = address(c, a_slot, 8)
        b_at = address(jnp.where(k8 < 4, 2 * c, 2 * c + 1), b_slot, 16)
        table[pl.ds(c * 8, 8), :] = jnp.where(live, a_at + b_at * 65536, 0)
        bit = jnp.where(live, lax.shift_left(one, k8 + 8 * (c % 4)), 0)
        if c < 4:
            low = low | bit
        else:
            high = high | bit
    for n, word in enumerate((low, high)):
        word = word | pltpu.roll(word, 4, 0)
        word = word | pltpu.roll(word, 2, 0)
        word = word | pltpu.roll(word, 1, 0)
        words[pl.ds(8 * n, 8), :] = jnp.where(k8 == 0, word, lax.population_count(word))
    t0 = pltpu.make_async_copy(table, table_s, sem_t.at[0])
    t1 = pltpu.make_async_copy(words, words_s, sem_t.at[1])
    t0.start()
    t1.start()
    t0.wait()
    t1.wait()

    def gather(p, total):
        for n in range(2):

            def one(m, bits):
                lowest = bits & -bits
                k = 31 - lax.clz(lowest) + 32 * n
                list_s[0, total + m] = table_s[k, p]
                list_s[1, total + m] = p
                return bits ^ lowest

            found = words_s[8 * n + 1, p]
            lax.fori_loop(0, found, one, words_s[8 * n, p])
            total = total + found
        return total

    def term(entry):
        a_at = pl.multiple_of((entry & 65535) * W, W)
        b_at = pl.multiple_of(lax.shift_right_logical(entry, 16) * W, W)
        a_high, a_low = split(a_all[pl.ds(a_at, W), :])
        b_high, b_low = split(b_all[pl.ds(b_at, W), :])
        left = jnp.concatenate([a_high, a_low], axis=1)
        right = jnp.concatenate(
            [jnp.concatenate([b_high, b_low], axis=1), jnp.concatenate([b_low, b_high], axis=1)], axis=0
        )
        both = jnp.dot(left, right, preferred_element_type=jnp.float32)
        return both[:, :W] + both[:, W:]

    def place(p):
        return pl.ds(pl.multiple_of(p // 8 * W, W), W), pl.ds(pl.multiple_of(p % 8 * W, W), W)

    total = lax.fori_loop(0, 32, gather, jnp.int32(0))

    def four(t, _):
        terms = [term(list_s[0, 4 * t + n]) for n in range(4)]
        for n in range(4):
            rows, cols = place(list_s[1, 4 * t + n])
            acc[rows, cols] = acc[rows, cols] + terms[n]
        return 0

    def single(t, _):
        rows, cols = place(list_s[1, t])
        acc[rows, cols] = acc[rows, cols] + term(list_s[0, t])
        return 0

    lax.fori_loop(0, total // 4, four, 0)
    lax.fori_loop(total // 4 * 4, total, single, 0)
    out = pltpu.make_async_copy(acc, out_ref, sem_o)
    out.start()
    out.wait()


def product(spread, where, keep_tile, groups):
    hbm = pl.BlockSpec(memory_space=pl.ANY)
    shapes = tuple(len(group) for group in groups)
    pieces = [piece for group in groups for piece in group]
    more = (8, 16) if spread else (1, 1)
    return pl.pallas_call(
        functools.partial(product_kernel, shapes, spread),
        out_shape=jax.ShapeDtypeStruct((512, 1024), jnp.float32),
        in_specs=[pl.BlockSpec(memory_space=pltpu.SMEM), pl.BlockSpec(memory_space=pltpu.VMEM)] + [hbm] * len(pieces),
        out_specs=hbm,
        scratch_shapes=[
            pltpu.VMEM((512, 1024), jnp.float32),
            pltpu.VMEM(((8 + more[0]) * DATA, W), jnp.float32),
            pltpu.VMEM(((16 + more[1]) * DATA, W), jnp.float32),
            pltpu.VMEM((64, W), jnp.float32),
            pltpu.VMEM((128, W), jnp.float32),
            pltpu.VMEM((64, W), jnp.int32),
            pltpu.VMEM((16, W), jnp.int32),
            pltpu.SMEM((64, W), jnp.int32),
            pltpu.SMEM((16, W), jnp.int32),
            pltpu.SMEM((2, 2048), jnp.int32),
            pltpu.SemaphoreType.DMA((72,)),
            pltpu.SemaphoreType.DMA((2,)),
            pltpu.SemaphoreType.DMA,
        ],
        compiler_params=pltpu.CompilerParams(vmem_limit_bytes=48 * 1024 * 1024),
        name="product",
    )(where, keep_tile, *pieces)


def swap(x, axis):
    return lax.ppermute(x, axis, [(0, 1), (1, 0)])


def right(x, axis):
    return lax.ppermute(x, axis, [(n, (n + 1) % 4) for n in range(4)])


def left(x, axis):
    return lax.ppermute(x, axis, [(n, (n - 1) % 4) for n in range(4)])


def opposite(from_left, from_right, core, axis):
    if axis == "x":
        axes, at = ("core", "x"), lambda n, c: c * 4 + n % 4
    else:
        axes, at = ("y", "core"), lambda n, c: n % 4 * 2 + c
    pairs = [(at(n, c), at(n + 1 - 2 * c, c)) for n in range(4) for c in range(2)]
    return lax.ppermute(jnp.where(core == 0, from_left, from_right), axes, pairs)


def gate(*done):
    return lambda x: lax.optimization_barrier((x, *done))[0]


def around(own, z, axis, core):
    other = swap(own, z)
    found = []
    for x in (own, other):
        r, l = right(x, axis), left(x, axis)
        found.extend((x, r, l, opposite(r, l, core, axis)))
    return found


SIZES = (2, 4, 2, 2, 4)


def route(x, ring, z):
    pairs = []
    for n in range(128):
        zl, y, core, zh, at = (int(i) for i in np.unravel_index(n, SIZES))
        if core == 0:
            to = (zl, y, core, zh ^ z, ring(at))
        else:
            to = (zl ^ z, ring(y), core, zh, at)
        pairs.append((n, int(np.ravel_multi_index(to, SIZES))))
    return lax.ppermute(x, ROW + COL, pairs)


def forth(x):
    return route(x, lambda n: (n + 1) % 4, 0)


def back(x):
    return route(x, lambda n: (n - 1) % 4, 0)


def cross(x):
    return route(x, lambda n: n, 1)


def pair(x, distance):
    return route(x, lambda n: n ^ distance, 0)


def per_device(a_values, a_mask, b_values, b_mask, keep):
    zl, y, core = (lax.axis_index(n) for n in ROW)
    zh, x = (lax.axis_index(n) for n in COL)
    core_s = core.reshape(1).astype(jnp.int32)
    keep_tile = jnp.pad(jnp.transpose(keep, (1, 0, 2)).reshape(64, 32), ((0, 0), (0, W - 32)))
    held, sent = pack(core_s, a_mask, b_mask, a_values, b_values)
    m, e = merge(core_s, held, swap(sent, "core"))

    r, l, z0 = forth(m), back(m), cross(m[:DATA])

    g = gate(r, l, z0)
    z1 = cross(g(m[DATA:]))
    o0, o1 = forth(g(r[:DATA])), back(g(l[DATA:]))
    e1 = pair(g(e), 1)
    cm = swap(g(m), "core")
    cr = swap(gate(cm)(g(r)), "core")
    cl = swap(gate(cr)(g(l)), "core")
    e = e + e1

    g = gate(z1, o0, o1, e1, cl)
    z = jnp.concatenate([g(z0), g(z1)])
    zr, zl_ = forth(z), back(z)
    e2 = cross(g(e))
    cz = swap(z, "core")
    co0 = swap(gate(cz)(g(o0)), "core")
    co1 = swap(gate(co0)(g(o1)), "core")
    e = e + e2

    g = gate(zr, zl_, e2, co1)
    zo0, zo1 = forth(g(zr[:DATA])), back(g(zl_[DATA:]))
    e3 = pair(g(e), 2)
    czr = swap(g(zr), "core")
    czl = swap(gate(czr)(g(zl_)), "core")
    e = e + e3

    g = gate(zo0, zo1, e3, czl)
    ce = swap(g(e), "core")
    czo0, czo1 = swap(g(zo0), "core"), swap(g(zo1), "core")

    shifts = (0, 3, 1, 2)
    groups = [[m], [cm], [r], [cr], [l], [cl], [o0, o1], [co0, co1]]
    groups += [[z], [cz], [zr], [czr], [zl_], [czl], [zo0, zo1], [czo0, czo1], [e, ce]]
    where = [core] + [(zh ^ n) * 4 + (x + s) % 4 for n in range(2) for s in shifts]
    where += [(zl ^ n) * 4 + (y + s) % 4 for n in range(2) for s in shifts]
    where = jnp.stack(where).astype(jnp.int32)
    crowd = [q[DATA, 0] > 1.5 for q in (e, ce)]

    def few(_):
        return product(False, where, keep_tile, groups)

    def many(_):
        first = core == 0
        crowd_a, crowd_b = jnp.where(first, crowd[0], crowd[1]), jnp.where(first, crowd[1], crowd[0])
        rest_a = jnp.where(first, held, sent)[DATA:TILES]
        rest_b = jnp.where(first, sent, held)[DATA:TILES]
        some_a = jnp.where(first, e, ce)[:DATA]
        some_b = jnp.where(first, ce, e)[:DATA]

        def all_b(_):
            found = around(rest_b, "zl", "y", core)
            return tuple(found + [swap(p, "core") for p in found])

        more = lax.cond(crowd_a, lambda _: tuple(around(rest_a, "zh", "x", core)), lambda _: (some_a,) * 8, 0)
        more += lax.cond(crowd_b, all_b, lambda _: (some_b,) * 16, 0)
        return product(True, where, keep_tile, groups + [[p] for p in more])

    return lax.cond(crowd[0] | crowd[1], many, few, 0)


def solution(mesh):
    fine = Mesh(mesh.devices.reshape(2, 4, 2, 2, 4), ROW + COL)
    return jax.shard_map(
        per_device,
        mesh=fine,
        in_specs=(P(ROW, COL), P(ROW, COL), P(ROW, COL), P(ROW, COL), P(ROW, None, COL)),
        out_specs=P(ROW, COL),
        check_vma=False,
    )
```

```python
import functools

import jax
import jax.numpy as jnp
import numpy as np
from jax import lax
from jax.experimental import pallas as pl
from jax.experimental.pallas import tpu as pltpu
from jax.sharding import Mesh
from jax.sharding import PartitionSpec as P

W = 128
SLOTS = 10
DATA = SLOTS * W
TILES = 2 * DATA
ROWS = TILES + 16
ROW = ("zl", "y", "core")
COL = ("zh", "x")


def pack_kernel(core_ref, am_ref, bm_ref, a_ref, b_ref, keep_ref, send_ref, sem):
    core = core_ref[0]
    row = lax.broadcasted_iota(jnp.int32, (8, W), 0)
    lane = lax.broadcasted_iota(jnp.int32, (8, W), 1)
    factors = (
        (am_ref, a_ref, lambda r, c: (row == c) & (lane // 8 == r)),
        (bm_ref, b_ref, lambda r, c: (row == r) & (lane % 8 == c)),
    )

    def copy(n, src, dst, r, c, cols, at):
        return pltpu.make_async_copy(
            src.at[pl.ds(r * W, W), pl.ds(c * W, W)], dst.at[pl.ds(at, W), :], sem.at[n * 32 + r * cols + c]
        )

    for n, (mask, src, spot) in enumerate(factors):
        rows, cols = mask.shape
        slot = jnp.int32(0)
        tile = jnp.zeros((8, W), jnp.float32)
        for r in range(rows):
            for c in range(cols):
                on = mask[r, c] != 0
                fits = on & (slot < 2 * SLOTS)
                at = pl.multiple_of(slot * W, W)
                for dst, here in ((keep_ref, core == n), (send_ref, core != n)):

                    @pl.when(fits & here)
                    def _():
                        copy(n, src, dst, r, c, cols, at).start()

                slot = slot + on.astype(jnp.int32)
                tile = jnp.where(spot(r, c), jnp.where(on, slot, 0).astype(jnp.float32), tile)
        flag = jnp.zeros((8, W), jnp.float32) + jnp.where(slot > SLOTS, 1.0, 0.0)
        for dst, here in ((keep_ref, core == n), (send_ref, core != n)):

            @pl.when(here)
            def _():
                dst[pl.ds(TILES, 8), :] = tile
                dst[pl.ds(TILES + 8, 8), :] = flag

    for n, (mask, src, _) in enumerate(factors):
        rows, cols = mask.shape
        for r in range(rows):
            for c in range(cols):

                @pl.when(mask[r, c] != 0)
                def _():
                    copy(n, src, keep_ref, r, c, cols, 0).wait()


def pack(core, a_mask, b_mask, a_values, b_values):
    smem = pl.BlockSpec(memory_space=pltpu.SMEM)
    vmem = pl.BlockSpec(memory_space=pltpu.VMEM)
    hbm = pl.BlockSpec(memory_space=pl.ANY)
    return pl.pallas_call(
        pack_kernel,
        out_shape=(jax.ShapeDtypeStruct((ROWS, W), jnp.float32),) * 2,
        in_specs=[smem, smem, smem, hbm, hbm],
        out_specs=(vmem,) * 2,
        scratch_shapes=[pltpu.SemaphoreType.DMA((64,))],
        name="pack",
    )(core, a_mask, b_mask, a_values, b_values)


def merge_kernel(core_ref, keep_ref, got_ref, main_ref, excess_ref):
    core = core_ref[0]
    for ref, at in ((keep_ref, core), (got_ref, 1 - core)):
        main_ref[pl.ds(pl.multiple_of(at * DATA, DATA), DATA), :] = ref[pl.ds(0, DATA), :]
        main_ref[pl.ds(pl.multiple_of(TILES + at * 8, 8), 8), :] = ref[pl.ds(TILES, 8), :]
    own = keep_ref[pl.ds(TILES + 8, 8), :]
    also = got_ref[pl.ds(TILES + 8, 8), :]
    kept = jnp.where(also[:1] > 0, got_ref[pl.ds(DATA, DATA), :], 0.0)
    excess_ref[pl.ds(0, DATA), :] = jnp.where(own[:1] > 0, keep_ref[pl.ds(DATA, DATA), :], kept)
    excess_ref[pl.ds(DATA, 8), :] = own + also


def merge(core, keep, got):
    vmem = pl.BlockSpec(memory_space=pltpu.VMEM)
    return pl.pallas_call(
        merge_kernel,
        out_shape=(
            jax.ShapeDtypeStruct((ROWS, W), jnp.float32),
            jax.ShapeDtypeStruct((DATA + 8, W), jnp.float32),
        ),
        in_specs=[pl.BlockSpec(memory_space=pltpu.SMEM), vmem, vmem],
        out_specs=(vmem, vmem),
        name="merge",
    )(core, keep, got)


def split(x):
    high = x.astype(jnp.bfloat16)
    low = (x - high.astype(jnp.float32)).astype(jnp.bfloat16)
    return high, low


def product_kernel(shapes, spread, where_ref, keep_ref, *refs):
    count = sum(shapes)
    pieces = list(refs[:count])
    out_ref, acc, a_all, b_all, a_meta, b_meta, table, words, table_s, words_s, list_s, sem, sem_t, sem_o = refs[count:]
    core = where_ref[0]
    groups = []
    for size in shapes:
        groups.append(pieces[:size])
        pieces = pieces[size:]
    lines, extra = groups[:17], groups[17:]

    def parts(piece):
        if len(piece) == 1:
            return [piece[0].at[pl.ds(0, DATA), :], piece[0].at[pl.ds(DATA, DATA), :], piece[0].at[pl.ds(TILES, 16), :]]
        return [piece[0], piece[1].at[pl.ds(0, DATA), :], piece[1].at[pl.ds(DATA, 16), :]]

    def copies(side):
        found = []
        for n in range(8):
            a_at, b_at = where_ref[1 + n], where_ref[9 + n]
            pair = (parts(lines[2 * n]), parts(lines[2 * n + 1]))
            a_parts, b_parts = pair[side], pair[1 - side]
            found.append((a_parts[side], a_all.at[pl.ds(a_at * DATA, DATA), :]))
            found.append((a_parts[2].at[pl.ds(8 * side, 8), :], a_meta.at[pl.ds(a_at * 8, 8), :]))
            for h in range(2):
                found.append((b_parts[h], b_all.at[pl.ds((b_at * 2 + h) * DATA, DATA), :]))
            found.append((b_parts[2], b_meta.at[pl.ds(b_at * 16, 16), :]))
        if not spread:
            e = lines[16]
            found.append((e[side].at[pl.ds(0, DATA), :], a_all.at[pl.ds(8 * DATA, DATA), :]))
            found.append((e[1 - side].at[pl.ds(0, DATA), :], b_all.at[pl.ds(16 * DATA, DATA), :]))
        for n, piece in enumerate(extra):
            if n < 8:
                found.append((piece[0], a_all.at[pl.ds((8 + where_ref[1 + n]) * DATA, DATA), :]))
            else:
                h = side if n < 16 else 1 - side
                at = 16 + where_ref[9 + n % 8] * 2 + h
                found.append((piece[0], b_all.at[pl.ds(at * DATA, DATA), :]))
        return [pltpu.make_async_copy(src, dst, sem.at[n]) for n, (src, dst) in enumerate(found)]

    for side in range(2):

        @pl.when(core == side)
        def _():
            for copy in copies(side):
                copy.start()

    acc[...] = jnp.zeros(acc.shape, jnp.float32)
    for side in range(2):

        @pl.when(core == side)
        def _():
            for copy in copies(side):
                copy.wait()

    def address(piece, rank, pieces):
        rest = pieces * SLOTS + rank - (SLOTS + 1)
        if spread:
            rest = rest + piece * SLOTS
        return jnp.where(rank <= SLOTS, piece * SLOTS + rank - 1, rest)

    k8 = lax.broadcasted_iota(jnp.int32, (8, W), 0)
    one = jnp.ones((8, W), jnp.int32)
    low = jnp.zeros((8, W), jnp.int32)
    high = jnp.zeros((8, W), jnp.int32)
    for c in range(8):
        a_slot = a_meta[pl.ds(c * 8, 8), :].astype(jnp.int32)
        b0 = b_meta[pl.ds(c * 16, 8), :].astype(jnp.int32)
        b1 = pltpu.roll(b_meta[pl.ds(c * 16 + 8, 8), :], 4, 0).astype(jnp.int32)
        b_slot = jnp.where(k8 < 4, b0, b1)
        live = (keep_ref[pl.ds(c * 8, 8), :] != 0) & (a_slot > 0) & (b_slot > 0)
        a_at = address(c, a_slot, 8)
        b_at = address(jnp.where(k8 < 4, 2 * c, 2 * c + 1), b_slot, 16)
        table[pl.ds(c * 8, 8), :] = jnp.where(live, a_at + b_at * 65536, 0)
        bit = jnp.where(live, lax.shift_left(one, k8 + 8 * (c % 4)), 0)
        if c < 4:
            low = low | bit
        else:
            high = high | bit
    for n, word in enumerate((low, high)):
        word = word | pltpu.roll(word, 4, 0)
        word = word | pltpu.roll(word, 2, 0)
        word = word | pltpu.roll(word, 1, 0)
        words[pl.ds(8 * n, 8), :] = jnp.where(k8 == 0, word, lax.population_count(word))
    t0 = pltpu.make_async_copy(table, table_s, sem_t.at[0])
    t1 = pltpu.make_async_copy(words, words_s, sem_t.at[1])
    t0.start()
    t1.start()
    t0.wait()
    t1.wait()

    def gather(p, total):
        for n in range(2):

            def one(m, bits):
                lowest = bits & -bits
                k = 31 - lax.clz(lowest) + 32 * n
                list_s[0, total + m] = table_s[k, p]
                list_s[1, total + m] = p
                return bits ^ lowest

            found = words_s[8 * n + 1, p]
            lax.fori_loop(0, found, one, words_s[8 * n, p])
            total = total + found
        return total

    def term(entry):
        a_at = pl.multiple_of((entry & 65535) * W, W)
        b_at = pl.multiple_of(lax.shift_right_logical(entry, 16) * W, W)
        a_high, a_low = split(a_all[pl.ds(a_at, W), :])
        b_high, b_low = split(b_all[pl.ds(b_at, W), :])
        left = jnp.concatenate([a_high, a_low], axis=1)
        right = jnp.concatenate(
            [jnp.concatenate([b_high, b_low], axis=1), jnp.concatenate([b_low, b_high], axis=1)], axis=0
        )
        both = jnp.dot(left, right, preferred_element_type=jnp.float32)
        return both[:, :W] + both[:, W:]

    def place(p):
        return pl.ds(pl.multiple_of(p // 8 * W, W), W), pl.ds(pl.multiple_of(p % 8 * W, W), W)

    total = lax.fori_loop(0, 32, gather, jnp.int32(0))

    def four(t, _):
        terms = [term(list_s[0, 4 * t + n]) for n in range(4)]
        for n in range(4):
            rows, cols = place(list_s[1, 4 * t + n])
            acc[rows, cols] = acc[rows, cols] + terms[n]
        return 0

    def single(t, _):
        rows, cols = place(list_s[1, t])
        acc[rows, cols] = acc[rows, cols] + term(list_s[0, t])
        return 0

    lax.fori_loop(0, total // 4, four, 0)
    lax.fori_loop(total // 4 * 4, total, single, 0)
    out = pltpu.make_async_copy(acc, out_ref, sem_o)
    out.start()
    out.wait()


def product(spread, where, keep_tile, groups):
    hbm = pl.BlockSpec(memory_space=pl.ANY)
    shapes = tuple(len(group) for group in groups)
    pieces = [piece for group in groups for piece in group]
    more = (8, 16) if spread else (1, 1)
    return pl.pallas_call(
        functools.partial(product_kernel, shapes, spread),
        out_shape=jax.ShapeDtypeStruct((512, 1024), jnp.float32),
        in_specs=[pl.BlockSpec(memory_space=pltpu.SMEM), pl.BlockSpec(memory_space=pltpu.VMEM)] + [hbm] * len(pieces),
        out_specs=hbm,
        scratch_shapes=[
            pltpu.VMEM((512, 1024), jnp.float32),
            pltpu.VMEM(((8 + more[0]) * DATA, W), jnp.float32),
            pltpu.VMEM(((16 + more[1]) * DATA, W), jnp.float32),
            pltpu.VMEM((64, W), jnp.float32),
            pltpu.VMEM((128, W), jnp.float32),
            pltpu.VMEM((64, W), jnp.int32),
            pltpu.VMEM((16, W), jnp.int32),
            pltpu.SMEM((64, W), jnp.int32),
            pltpu.SMEM((16, W), jnp.int32),
            pltpu.SMEM((2, 2048), jnp.int32),
            pltpu.SemaphoreType.DMA((72,)),
            pltpu.SemaphoreType.DMA((2,)),
            pltpu.SemaphoreType.DMA,
        ],
        compiler_params=pltpu.CompilerParams(vmem_limit_bytes=(40 if spread else 24) * 1024 * 1024),
        name="product",
    )(where, keep_tile, *pieces)


def swap(x, axis):
    return lax.ppermute(x, axis, [(0, 1), (1, 0)])


def right(x, axis):
    return lax.ppermute(x, axis, [(n, (n + 1) % 4) for n in range(4)])


def left(x, axis):
    return lax.ppermute(x, axis, [(n, (n - 1) % 4) for n in range(4)])


def opposite(from_left, from_right, core, axis):
    if axis == "x":
        axes, at = ("core", "x"), lambda n, c: c * 4 + n % 4
    else:
        axes, at = ("y", "core"), lambda n, c: n % 4 * 2 + c
    pairs = [(at(n, c), at(n + 1 - 2 * c, c)) for n in range(4) for c in range(2)]
    return lax.ppermute(jnp.where(core == 0, from_left, from_right), axes, pairs)


def gate(*done):
    return lambda x: lax.optimization_barrier((x, *done))[0]


def around(own, z, axis, core):
    other = swap(own, z)
    found = []
    for x in (own, other):
        r, l = right(x, axis), left(x, axis)
        found.extend((x, r, l, opposite(r, l, core, axis)))
    return found


SIZES = (2, 4, 2, 2, 4)


def route(x, ring, z):
    pairs = []
    for n in range(128):
        zl, y, core, zh, at = (int(i) for i in np.unravel_index(n, SIZES))
        if core == 0:
            to = (zl, y, core, zh ^ z, ring(at))
        else:
            to = (zl ^ z, ring(y), core, zh, at)
        pairs.append((n, int(np.ravel_multi_index(to, SIZES))))
    return lax.ppermute(x, ROW + COL, pairs)


def forth(x):
    return route(x, lambda n: (n + 1) % 4, 0)


def back(x):
    return route(x, lambda n: (n - 1) % 4, 0)


def cross(x):
    return route(x, lambda n: n, 1)


def pair(x, distance):
    return route(x, lambda n: n ^ distance, 0)


def per_device(a_values, a_mask, b_values, b_mask, keep):
    zl, y, core = (lax.axis_index(n) for n in ROW)
    zh, x = (lax.axis_index(n) for n in COL)
    core_s = core.reshape(1).astype(jnp.int32)
    keep_tile = jnp.pad(jnp.transpose(keep, (1, 0, 2)).reshape(64, 32), ((0, 0), (0, W - 32)))
    held, sent = pack(core_s, a_mask, b_mask, a_values, b_values)
    m, e = merge(core_s, held, swap(sent, "core"))

    z0 = cross(m[:DATA])
    r, l = forth(m), back(m)
    cm = swap(m, "core")
    z1 = cross(gate(z0, r, l)(m[DATA:]))
    o0, o1 = forth(r[:DATA]), back(l[DATA:])
    e1 = pair(gate(r, l)(e), 1)
    cr, cl = swap(r, "core"), swap(l, "core")
    e = e + e1

    g = gate(o0, o1)
    z = jnp.concatenate([g(z0), g(z1)])
    zr, zl_ = forth(z), back(z)
    e2 = cross(gate(z1)(e))
    cz, co0, co1 = swap(z, "core"), swap(o0, "core"), swap(o1, "core")
    e = e + e2

    zo0, zo1 = forth(zr[:DATA]), back(zl_[DATA:])
    e3 = pair(gate(zr, zl_)(e), 2)
    czr, czl = swap(zr, "core"), swap(zl_, "core")
    e = e + e3
    ce = swap(e, "core")
    czo0, czo1 = swap(zo0, "core"), swap(zo1, "core")

    shifts = (0, 3, 1, 2)
    groups = [[m], [cm], [r], [cr], [l], [cl], [o0, o1], [co0, co1]]
    groups += [[z], [cz], [zr], [czr], [zl_], [czl], [zo0, zo1], [czo0, czo1], [e, ce]]
    where = [core] + [(zh ^ n) * 4 + (x + s) % 4 for n in range(2) for s in shifts]
    where += [(zl ^ n) * 4 + (y + s) % 4 for n in range(2) for s in shifts]
    where = jnp.stack(where).astype(jnp.int32)
    crowd = [q[DATA, 0] > 1.5 for q in (e, ce)]

    def few(_):
        return product(False, where, keep_tile, groups)

    def many(_):
        first = core == 0
        crowd_a, crowd_b = jnp.where(first, crowd[0], crowd[1]), jnp.where(first, crowd[1], crowd[0])
        rest_a = jnp.where(first, held, sent)[DATA:TILES]
        rest_b = jnp.where(first, sent, held)[DATA:TILES]
        some_a = jnp.where(first, e, ce)[:DATA]
        some_b = jnp.where(first, ce, e)[:DATA]

        def all_b(_):
            found = around(rest_b, "zl", "y", core)
            return tuple(found + [swap(p, "core") for p in found])

        more = lax.cond(crowd_a, lambda _: tuple(around(rest_a, "zh", "x", core)), lambda _: (some_a,) * 8, 0)
        more += lax.cond(crowd_b, all_b, lambda _: (some_b,) * 16, 0)
        return product(True, where, keep_tile, groups + [[p] for p in more])

    return lax.cond(crowd[0] | crowd[1], many, few, 0)


def solution(mesh):
    fine = Mesh(mesh.devices.reshape(2, 4, 2, 2, 4), ROW + COL)
    return jax.shard_map(
        per_device,
        mesh=fine,
        in_specs=(P(ROW, COL), P(ROW, COL), P(ROW, COL), P(ROW, COL), P(ROW, None, COL)),
        out_specs=P(ROW, COL),
        check_vma=False,
    )
```

```python
import functools

import jax
import jax.numpy as jnp
import numpy as np
from jax import lax
from jax.experimental import pallas as pl
from jax.experimental.pallas import tpu as pltpu
from jax.sharding import Mesh
from jax.sharding import PartitionSpec as P

W = 128
SLOTS = 10
DATA = SLOTS * W
TILES = 2 * DATA
ROWS = TILES + 16
ROW = ("zl", "y", "core")
COL = ("zh", "x")


def pack_kernel(core_ref, am_ref, bm_ref, a_ref, b_ref, keep_ref, send_ref, sem):
    core = core_ref[0]
    row = lax.broadcasted_iota(jnp.int32, (8, W), 0)
    lane = lax.broadcasted_iota(jnp.int32, (8, W), 1)
    factors = (
        (am_ref, a_ref, lambda r, c: (row == c) & (lane // 8 == r)),
        (bm_ref, b_ref, lambda r, c: (row == r) & (lane % 8 == c)),
    )

    def copy(n, src, dst, r, c, cols, at):
        return pltpu.make_async_copy(
            src.at[pl.ds(r * W, W), pl.ds(c * W, W)], dst.at[pl.ds(at, W), :], sem.at[n * 32 + r * cols + c]
        )

    for n, (mask, src, spot) in enumerate(factors):
        rows, cols = mask.shape
        slot = jnp.int32(0)
        tile = jnp.zeros((8, W), jnp.float32)
        for r in range(rows):
            for c in range(cols):
                on = mask[r, c] != 0
                fits = on & (slot < 2 * SLOTS)
                at = pl.multiple_of(slot * W, W)
                for dst, here in ((keep_ref, core == n), (send_ref, core != n)):

                    @pl.when(fits & here)
                    def _():
                        copy(n, src, dst, r, c, cols, at).start()

                slot = slot + on.astype(jnp.int32)
                tile = jnp.where(spot(r, c), jnp.where(on, slot, 0).astype(jnp.float32), tile)
        flag = jnp.zeros((8, W), jnp.float32) + jnp.where(slot > SLOTS, 1.0, 0.0)
        for dst, here in ((keep_ref, core == n), (send_ref, core != n)):

            @pl.when(here)
            def _():
                dst[pl.ds(TILES, 8), :] = tile
                dst[pl.ds(TILES + 8, 8), :] = flag

    for n, (mask, src, _) in enumerate(factors):
        rows, cols = mask.shape
        for r in range(rows):
            for c in range(cols):

                @pl.when(mask[r, c] != 0)
                def _():
                    copy(n, src, keep_ref, r, c, cols, 0).wait()


def pack(core, a_mask, b_mask, a_values, b_values):
    smem = pl.BlockSpec(memory_space=pltpu.SMEM)
    vmem = pl.BlockSpec(memory_space=pltpu.VMEM)
    hbm = pl.BlockSpec(memory_space=pl.ANY)
    return pl.pallas_call(
        pack_kernel,
        out_shape=(jax.ShapeDtypeStruct((ROWS, W), jnp.float32),) * 2,
        in_specs=[smem, smem, smem, hbm, hbm],
        out_specs=(vmem,) * 2,
        scratch_shapes=[pltpu.SemaphoreType.DMA((64,))],
        name="pack",
    )(core, a_mask, b_mask, a_values, b_values)


def merge_kernel(core_ref, keep_ref, got_ref, main_ref, excess_ref):
    core = core_ref[0]
    for ref, at in ((keep_ref, core), (got_ref, 1 - core)):
        main_ref[pl.ds(pl.multiple_of(at * DATA, DATA), DATA), :] = ref[pl.ds(0, DATA), :]
        main_ref[pl.ds(pl.multiple_of(TILES + at * 8, 8), 8), :] = ref[pl.ds(TILES, 8), :]
    own = keep_ref[pl.ds(TILES + 8, 8), :]
    also = got_ref[pl.ds(TILES + 8, 8), :]
    kept = jnp.where(also[:1] > 0, got_ref[pl.ds(DATA, DATA), :], 0.0)
    excess_ref[pl.ds(0, DATA), :] = jnp.where(own[:1] > 0, keep_ref[pl.ds(DATA, DATA), :], kept)
    excess_ref[pl.ds(DATA, 8), :] = own + also


def merge(core, keep, got):
    vmem = pl.BlockSpec(memory_space=pltpu.VMEM)
    return pl.pallas_call(
        merge_kernel,
        out_shape=(
            jax.ShapeDtypeStruct((ROWS, W), jnp.float32),
            jax.ShapeDtypeStruct((DATA + 8, W), jnp.float32),
        ),
        in_specs=[pl.BlockSpec(memory_space=pltpu.SMEM), vmem, vmem],
        out_specs=(vmem, vmem),
        name="merge",
    )(core, keep, got)


def split(x):
    high = x.astype(jnp.bfloat16)
    low = (x - high.astype(jnp.float32)).astype(jnp.bfloat16)
    return high, low


def product_kernel(shapes, spread, where_ref, keep_ref, *refs):
    count = sum(shapes)
    pieces = list(refs[:count])
    out_ref, acc, a_all, b_all, a_meta, b_meta, table, words, table_s, words_s, list_s, sem, sem_t, sem_o = refs[count:]
    core = where_ref[0]
    groups = []
    for size in shapes:
        groups.append(pieces[:size])
        pieces = pieces[size:]
    lines, extra = groups[:17], groups[17:]

    def parts(piece):
        if len(piece) == 1:
            return [piece[0].at[pl.ds(0, DATA), :], piece[0].at[pl.ds(DATA, DATA), :], piece[0].at[pl.ds(TILES, 16), :]]
        return [piece[0], piece[1].at[pl.ds(0, DATA), :], piece[1].at[pl.ds(DATA, 16), :]]

    def copies(side):
        found = []
        for n in range(8):
            a_at, b_at = where_ref[1 + n], where_ref[9 + n]
            pair = (parts(lines[2 * n]), parts(lines[2 * n + 1]))
            a_parts, b_parts = pair[side], pair[1 - side]
            found.append((a_parts[side], a_all.at[pl.ds(a_at * DATA, DATA), :]))
            found.append((a_parts[2].at[pl.ds(8 * side, 8), :], a_meta.at[pl.ds(a_at * 8, 8), :]))
            for h in range(2):
                found.append((b_parts[h], b_all.at[pl.ds((b_at * 2 + h) * DATA, DATA), :]))
            found.append((b_parts[2], b_meta.at[pl.ds(b_at * 16, 16), :]))
        if not spread:
            e = lines[16]
            found.append((e[side].at[pl.ds(0, DATA), :], a_all.at[pl.ds(8 * DATA, DATA), :]))
            found.append((e[1 - side].at[pl.ds(0, DATA), :], b_all.at[pl.ds(16 * DATA, DATA), :]))
        for n, piece in enumerate(extra):
            if n < 8:
                found.append((piece[0], a_all.at[pl.ds((8 + where_ref[1 + n]) * DATA, DATA), :]))
            else:
                h = side if n < 16 else 1 - side
                at = 16 + where_ref[9 + n % 8] * 2 + h
                found.append((piece[0], b_all.at[pl.ds(at * DATA, DATA), :]))
        found.sort(key=lambda pair: pair[0].shape[0] >= DATA)
        small = sum(pair[0].shape[0] < DATA for pair in found)
        made = [pltpu.make_async_copy(src, dst, sem.at[n]) for n, (src, dst) in enumerate(found)]
        return made, made[:small], made[small:]

    for side in range(2):

        @pl.when(core == side)
        def _():
            for copy in copies(side)[0]:
                copy.start()

    def settle(which):
        for side in range(2):

            @pl.when(core == side)
            def _():
                for copy in copies(side)[which]:
                    copy.wait()

    acc[...] = jnp.zeros(acc.shape, jnp.float32)
    settle(1)

    def address(piece, rank, pieces):
        rest = pieces * SLOTS + rank - (SLOTS + 1)
        if spread:
            rest = rest + piece * SLOTS
        return jnp.where(rank <= SLOTS, piece * SLOTS + rank - 1, rest)

    k8 = lax.broadcasted_iota(jnp.int32, (8, W), 0)
    one = jnp.ones((8, W), jnp.int32)
    low = jnp.zeros((8, W), jnp.int32)
    high = jnp.zeros((8, W), jnp.int32)
    for c in range(8):
        a_slot = a_meta[pl.ds(c * 8, 8), :].astype(jnp.int32)
        b0 = b_meta[pl.ds(c * 16, 8), :].astype(jnp.int32)
        b1 = pltpu.roll(b_meta[pl.ds(c * 16 + 8, 8), :], 4, 0).astype(jnp.int32)
        b_slot = jnp.where(k8 < 4, b0, b1)
        live = (keep_ref[pl.ds(c * 8, 8), :] != 0) & (a_slot > 0) & (b_slot > 0)
        a_at = address(c, a_slot, 8)
        b_at = address(jnp.where(k8 < 4, 2 * c, 2 * c + 1), b_slot, 16)
        table[pl.ds(c * 8, 8), :] = jnp.where(live, a_at + b_at * 65536, 0)
        bit = jnp.where(live, lax.shift_left(one, k8 + 8 * (c % 4)), 0)
        if c < 4:
            low = low | bit
        else:
            high = high | bit
    for n, word in enumerate((low, high)):
        word = word | pltpu.roll(word, 4, 0)
        word = word | pltpu.roll(word, 2, 0)
        word = word | pltpu.roll(word, 1, 0)
        words[pl.ds(8 * n, 8), :] = jnp.where(k8 == 0, word, lax.population_count(word))
    t0 = pltpu.make_async_copy(table, table_s, sem_t.at[0])
    t1 = pltpu.make_async_copy(words, words_s, sem_t.at[1])
    t0.start()
    t1.start()
    t0.wait()
    t1.wait()

    def gather(p, total):
        for n in range(2):

            def one(m, bits):
                lowest = bits & -bits
                k = 31 - lax.clz(lowest) + 32 * n
                list_s[0, total + m] = table_s[k, p]
                list_s[1, total + m] = p
                return bits ^ lowest

            found = words_s[8 * n + 1, p]
            lax.fori_loop(0, found, one, words_s[8 * n, p])
            total = total + found
        return total

    def term(entry):
        a_at = pl.multiple_of((entry & 65535) * W, W)
        b_at = pl.multiple_of(lax.shift_right_logical(entry, 16) * W, W)
        a_high, a_low = split(a_all[pl.ds(a_at, W), :])
        b_high, b_low = split(b_all[pl.ds(b_at, W), :])
        left = jnp.concatenate([a_high, a_low], axis=1)
        right = jnp.concatenate(
            [jnp.concatenate([b_high, b_low], axis=1), jnp.concatenate([b_low, b_high], axis=1)], axis=0
        )
        both = jnp.dot(left, right, preferred_element_type=jnp.float32)
        return both[:, :W] + both[:, W:]

    def place(p):
        return pl.ds(pl.multiple_of(p // 8 * W, W), W), pl.ds(pl.multiple_of(p % 8 * W, W), W)

    total = lax.fori_loop(0, 32, gather, jnp.int32(0))
    settle(2)

    def four(t, _):
        terms = [term(list_s[0, 4 * t + n]) for n in range(4)]
        for n in range(4):
            rows, cols = place(list_s[1, 4 * t + n])
            acc[rows, cols] = acc[rows, cols] + terms[n]
        return 0

    def single(t, _):
        rows, cols = place(list_s[1, t])
        acc[rows, cols] = acc[rows, cols] + term(list_s[0, t])
        return 0

    lax.fori_loop(0, total // 4, four, 0)
    lax.fori_loop(total // 4 * 4, total, single, 0)
    out = pltpu.make_async_copy(acc, out_ref, sem_o)
    out.start()
    out.wait()


def product(spread, where, keep_tile, groups):
    hbm = pl.BlockSpec(memory_space=pl.ANY)
    shapes = tuple(len(group) for group in groups)
    pieces = [piece for group in groups for piece in group]
    more = (8, 16) if spread else (1, 1)
    return pl.pallas_call(
        functools.partial(product_kernel, shapes, spread),
        out_shape=jax.ShapeDtypeStruct((512, 1024), jnp.float32),
        in_specs=[pl.BlockSpec(memory_space=pltpu.SMEM), pl.BlockSpec(memory_space=pltpu.VMEM)] + [hbm] * len(pieces),
        out_specs=hbm,
        scratch_shapes=[
            pltpu.VMEM((512, 1024), jnp.float32),
            pltpu.VMEM(((8 + more[0]) * DATA, W), jnp.float32),
            pltpu.VMEM(((16 + more[1]) * DATA, W), jnp.float32),
            pltpu.VMEM((64, W), jnp.float32),
            pltpu.VMEM((128, W), jnp.float32),
            pltpu.VMEM((64, W), jnp.int32),
            pltpu.VMEM((16, W), jnp.int32),
            pltpu.SMEM((64, W), jnp.int32),
            pltpu.SMEM((16, W), jnp.int32),
            pltpu.SMEM((2, 2048), jnp.int32),
            pltpu.SemaphoreType.DMA((72,)),
            pltpu.SemaphoreType.DMA((2,)),
            pltpu.SemaphoreType.DMA,
        ],
        compiler_params=pltpu.CompilerParams(vmem_limit_bytes=(40 if spread else 24) * 1024 * 1024),
        name="product",
    )(where, keep_tile, *pieces)


def swap(x, axis):
    return lax.ppermute(x, axis, [(0, 1), (1, 0)])


def right(x, axis):
    return lax.ppermute(x, axis, [(n, (n + 1) % 4) for n in range(4)])


def left(x, axis):
    return lax.ppermute(x, axis, [(n, (n - 1) % 4) for n in range(4)])


def opposite(from_left, from_right, core, axis):
    if axis == "x":
        axes, at = ("core", "x"), lambda n, c: c * 4 + n % 4
    else:
        axes, at = ("y", "core"), lambda n, c: n % 4 * 2 + c
    pairs = [(at(n, c), at(n + 1 - 2 * c, c)) for n in range(4) for c in range(2)]
    return lax.ppermute(jnp.where(core == 0, from_left, from_right), axes, pairs)


def gate(*done):
    return lambda x: lax.optimization_barrier((x, *done))[0]


def around(own, z, axis, core):
    other = swap(own, z)
    found = []
    for x in (own, other):
        r, l = right(x, axis), left(x, axis)
        found.extend((x, r, l, opposite(r, l, core, axis)))
    return found


SIZES = (2, 4, 2, 2, 4)


def route(x, ring, z):
    pairs = []
    for n in range(128):
        zl, y, core, zh, at = (int(i) for i in np.unravel_index(n, SIZES))
        if core == 0:
            to = (zl, y, core, zh ^ z, ring(at))
        else:
            to = (zl ^ z, ring(y), core, zh, at)
        pairs.append((n, int(np.ravel_multi_index(to, SIZES))))
    return lax.ppermute(x, ROW + COL, pairs)


def forth(x):
    return route(x, lambda n: (n + 1) % 4, 0)


def back(x):
    return route(x, lambda n: (n - 1) % 4, 0)


def cross(x):
    return route(x, lambda n: n, 1)


def pair(x, distance):
    return route(x, lambda n: n ^ distance, 0)


def per_device(a_values, a_mask, b_values, b_mask, keep):
    zl, y, core = (lax.axis_index(n) for n in ROW)
    zh, x = (lax.axis_index(n) for n in COL)
    core_s = core.reshape(1).astype(jnp.int32)
    keep_tile = jnp.pad(jnp.transpose(keep, (1, 0, 2)).reshape(64, 32), ((0, 0), (0, W - 32)))
    held, sent = pack(core_s, a_mask, b_mask, a_values, b_values)
    m, e = merge(core_s, held, swap(sent, "core"))

    z0 = cross(m[:DATA])
    r, l = forth(m), back(m)
    e1 = pair(e, 1)
    cm = swap(m, "core")

    g = gate(r, l, z0)
    z1 = cross(g(m[DATA:]))
    o0, o1 = forth(g(r[:DATA])), back(g(l[DATA:]))
    z0r, z0l = forth(g(z0)), back(g(z0))
    e = g(e) + e1
    e2 = pair(e, 2)
    cr, cl = swap(r, "core"), swap(l, "core")

    g = gate(z1, z0r, z0l)
    z1r, z1l = forth(g(z1)), back(g(z1))
    zo0 = forth(g(z0r))
    e = g(e) + e2
    e3 = cross(e)
    cz0, co0, co1 = swap(z0, "core"), swap(o0, "core"), swap(o1, "core")
    cz0r, cz0l = swap(z0r, "core"), swap(z0l, "core")

    g = gate(z1r, z1l, cm, cr, cl, co0, co1, cz0)
    zo1 = back(g(z1l))
    e = g(e) + e3
    cz1, cz1r, cz1l = swap(z1, "core"), swap(z1r, "core"), swap(z1l, "core")
    czo0 = swap(zo0, "core")
    ce = swap(e, "core")
    czo1 = swap(zo1, "core")

    shifts = (0, 3, 1, 2)
    groups = [[m], [cm], [r], [cr], [l], [cl], [o0, o1], [co0, co1]]
    groups += [[z0, z1], [cz0, cz1], [z0r, z1r], [cz0r, cz1r], [z0l, z1l], [cz0l, cz1l], [zo0, zo1], [czo0, czo1], [e, ce]]
    where = [core] + [(zh ^ n) * 4 + (x + s) % 4 for n in range(2) for s in shifts]
    where += [(zl ^ n) * 4 + (y + s) % 4 for n in range(2) for s in shifts]
    where = jnp.stack(where).astype(jnp.int32)
    crowd = [q[DATA, 0] > 1.5 for q in (e, ce)]

    def few(_):
        return product(False, where, keep_tile, groups)

    def many(_):
        first = core == 0
        crowd_a, crowd_b = jnp.where(first, crowd[0], crowd[1]), jnp.where(first, crowd[1], crowd[0])
        rest_a = jnp.where(first, held, sent)[DATA:TILES]
        rest_b = jnp.where(first, sent, held)[DATA:TILES]
        some_a = jnp.where(first, e, ce)[:DATA]
        some_b = jnp.where(first, ce, e)[:DATA]

        def all_b(_):
            found = around(rest_b, "zl", "y", core)
            return tuple(found + [swap(p, "core") for p in found])

        more = lax.cond(crowd_a, lambda _: tuple(around(rest_a, "zh", "x", core)), lambda _: (some_a,) * 8, 0)
        more += lax.cond(crowd_b, all_b, lambda _: (some_b,) * 16, 0)
        return product(True, where, keep_tile, groups + [[p] for p in more])

    return lax.cond(crowd[0] | crowd[1], many, few, 0)


def solution(mesh):
    fine = Mesh(mesh.devices.reshape(2, 4, 2, 2, 4), ROW + COL)
    return jax.shard_map(
        per_device,
        mesh=fine,
        in_specs=(P(ROW, COL), P(ROW, COL), P(ROW, COL), P(ROW, COL), P(ROW, None, COL)),
        out_specs=P(ROW, COL),
        check_vma=False,
    )
```

```python
import functools

import jax
import jax.numpy as jnp
import numpy as np
from jax import lax
from jax.experimental import pallas as pl
from jax.experimental.pallas import tpu as pltpu
from jax.sharding import Mesh
from jax.sharding import PartitionSpec as P

W = 128
SLOTS = 10
DATA = SLOTS * W
TILES = 2 * DATA
ROWS = TILES + 16
ROW = ("zl", "y", "core")
COL = ("zh", "x")


def pack_kernel(core_ref, am_ref, bm_ref, a_ref, b_ref, keep_ref, send_ref, sem):
    core = core_ref[0]
    row = lax.broadcasted_iota(jnp.int32, (8, W), 0)
    lane = lax.broadcasted_iota(jnp.int32, (8, W), 1)
    factors = (
        (am_ref, a_ref, lambda r, c: (row == c) & (lane // 8 == r)),
        (bm_ref, b_ref, lambda r, c: (row == r) & (lane % 8 == c)),
    )

    def copy(n, src, dst, r, c, cols, at):
        return pltpu.make_async_copy(
            src.at[pl.ds(r * W, W), pl.ds(c * W, W)], dst.at[pl.ds(at, W), :], sem.at[n * 32 + r * cols + c]
        )

    for n, (mask, src, spot) in enumerate(factors):
        rows, cols = mask.shape
        slot = jnp.int32(0)
        tile = jnp.zeros((8, W), jnp.float32)
        for r in range(rows):
            for c in range(cols):
                on = mask[r, c] != 0
                fits = on & (slot < 2 * SLOTS)
                at = pl.multiple_of(slot * W, W)
                for dst, here in ((keep_ref, core == n), (send_ref, core != n)):

                    @pl.when(fits & here)
                    def _():
                        copy(n, src, dst, r, c, cols, at).start()

                slot = slot + on.astype(jnp.int32)
                tile = jnp.where(spot(r, c), jnp.where(on, slot, 0).astype(jnp.float32), tile)
        flag = jnp.zeros((8, W), jnp.float32) + jnp.where(slot > SLOTS, 1.0, 0.0)
        for dst, here in ((keep_ref, core == n), (send_ref, core != n)):

            @pl.when(here)
            def _():
                dst[pl.ds(TILES, 8), :] = tile
                dst[pl.ds(TILES + 8, 8), :] = flag

    for n, (mask, src, _) in enumerate(factors):
        rows, cols = mask.shape
        for r in range(rows):
            for c in range(cols):

                @pl.when(mask[r, c] != 0)
                def _():
                    copy(n, src, keep_ref, r, c, cols, 0).wait()


def pack(core, a_mask, b_mask, a_values, b_values):
    smem = pl.BlockSpec(memory_space=pltpu.SMEM)
    vmem = pl.BlockSpec(memory_space=pltpu.VMEM)
    hbm = pl.BlockSpec(memory_space=pl.ANY)
    return pl.pallas_call(
        pack_kernel,
        out_shape=(jax.ShapeDtypeStruct((ROWS, W), jnp.float32),) * 2,
        in_specs=[smem, smem, smem, hbm, hbm],
        out_specs=(vmem,) * 2,
        scratch_shapes=[pltpu.SemaphoreType.DMA((64,))],
        name="pack",
    )(core, a_mask, b_mask, a_values, b_values)


def merge_kernel(core_ref, keep_ref, got_ref, main_ref, excess_ref):
    core = core_ref[0]
    for ref, at in ((keep_ref, core), (got_ref, 1 - core)):
        main_ref[pl.ds(pl.multiple_of(at * DATA, DATA), DATA), :] = ref[pl.ds(0, DATA), :]
        main_ref[pl.ds(pl.multiple_of(TILES + at * 8, 8), 8), :] = ref[pl.ds(TILES, 8), :]
    own = keep_ref[pl.ds(TILES + 8, 8), :]
    also = got_ref[pl.ds(TILES + 8, 8), :]
    kept = jnp.where(also[:1] > 0, got_ref[pl.ds(DATA, DATA), :], 0.0)
    excess_ref[pl.ds(0, DATA), :] = jnp.where(own[:1] > 0, keep_ref[pl.ds(DATA, DATA), :], kept)
    excess_ref[pl.ds(DATA, 8), :] = own + also


def merge(core, keep, got):
    vmem = pl.BlockSpec(memory_space=pltpu.VMEM)
    return pl.pallas_call(
        merge_kernel,
        out_shape=(
            jax.ShapeDtypeStruct((ROWS, W), jnp.float32),
            jax.ShapeDtypeStruct((DATA + 8, W), jnp.float32),
        ),
        in_specs=[pl.BlockSpec(memory_space=pltpu.SMEM), vmem, vmem],
        out_specs=(vmem, vmem),
        name="merge",
    )(core, keep, got)


def split(x):
    high = x.astype(jnp.bfloat16)
    low = (x - high.astype(jnp.float32)).astype(jnp.bfloat16)
    return high, low


def product_kernel(shapes, spread, where_ref, keep_ref, *refs):
    count = sum(shapes)
    pieces = list(refs[:count])
    out_ref, acc, a_all, b_all, a_meta, b_meta, table, words, table_s, words_s, list_s, sem, sem_t, sem_o = refs[count:]
    core = where_ref[0]
    groups = []
    for size in shapes:
        groups.append(pieces[:size])
        pieces = pieces[size:]
    lines, extra = groups[:17], groups[17:]

    def parts(piece):
        if len(piece) == 1:
            return [piece[0].at[pl.ds(0, DATA), :], piece[0].at[pl.ds(DATA, DATA), :], piece[0].at[pl.ds(TILES, 16), :]]
        return [piece[0], piece[1].at[pl.ds(0, DATA), :], piece[1].at[pl.ds(DATA, 16), :]]

    def copies(side):
        found = []
        for n in range(8):
            a_at, b_at = where_ref[1 + n], where_ref[9 + n]
            pair = (parts(lines[2 * n]), parts(lines[2 * n + 1]))
            a_parts, b_parts = pair[side], pair[1 - side]
            found.append((a_parts[side], a_all.at[pl.ds(a_at * DATA, DATA), :]))
            found.append((a_parts[2].at[pl.ds(8 * side, 8), :], a_meta.at[pl.ds(a_at * 8, 8), :]))
            for h in range(2):
                found.append((b_parts[h], b_all.at[pl.ds((b_at * 2 + h) * DATA, DATA), :]))
            found.append((b_parts[2], b_meta.at[pl.ds(b_at * 16, 16), :]))
        if not spread:
            e = lines[16]
            found.append((e[side].at[pl.ds(0, DATA), :], a_all.at[pl.ds(8 * DATA, DATA), :]))
            found.append((e[1 - side].at[pl.ds(0, DATA), :], b_all.at[pl.ds(16 * DATA, DATA), :]))
        for n, piece in enumerate(extra):
            if n < 8:
                found.append((piece[0], a_all.at[pl.ds((8 + where_ref[1 + n]) * DATA, DATA), :]))
            else:
                h = side if n < 16 else 1 - side
                at = 16 + where_ref[9 + n % 8] * 2 + h
                found.append((piece[0], b_all.at[pl.ds(at * DATA, DATA), :]))
        found.sort(key=lambda pair: pair[0].shape[0] >= DATA)
        small = sum(pair[0].shape[0] < DATA for pair in found)
        made = [pltpu.make_async_copy(src, dst, sem.at[n]) for n, (src, dst) in enumerate(found)]
        return made, made[:small], made[small:]

    for side in range(2):

        @pl.when(core == side)
        def _():
            for copy in copies(side)[0]:
                copy.start()

    def settle(which):
        for side in range(2):

            @pl.when(core == side)
            def _():
                for copy in copies(side)[which]:
                    copy.wait()

    acc[...] = jnp.zeros(acc.shape, jnp.float32)
    settle(1)

    def address(piece, rank, pieces):
        rest = pieces * SLOTS + rank - (SLOTS + 1)
        if spread:
            rest = rest + piece * SLOTS
        return jnp.where(rank <= SLOTS, piece * SLOTS + rank - 1, rest)

    k8 = lax.broadcasted_iota(jnp.int32, (8, W), 0)
    one = jnp.ones((8, W), jnp.int32)
    low = jnp.zeros((8, W), jnp.int32)
    high = jnp.zeros((8, W), jnp.int32)
    for c in range(8):
        a_slot = a_meta[pl.ds(c * 8, 8), :].astype(jnp.int32)
        b0 = b_meta[pl.ds(c * 16, 8), :].astype(jnp.int32)
        b1 = pltpu.roll(b_meta[pl.ds(c * 16 + 8, 8), :], 4, 0).astype(jnp.int32)
        b_slot = jnp.where(k8 < 4, b0, b1)
        live = (keep_ref[pl.ds(c * 8, 8), :] != 0) & (a_slot > 0) & (b_slot > 0)
        a_at = address(c, a_slot, 8)
        b_at = address(jnp.where(k8 < 4, 2 * c, 2 * c + 1), b_slot, 16)
        table[pl.ds(c * 8, 8), :] = jnp.where(live, a_at + b_at * 65536, 0)
        bit = jnp.where(live, lax.shift_left(one, k8 + 8 * (c % 4)), 0)
        if c < 4:
            low = low | bit
        else:
            high = high | bit
    for n, word in enumerate((low, high)):
        word = word | pltpu.roll(word, 4, 0)
        word = word | pltpu.roll(word, 2, 0)
        word = word | pltpu.roll(word, 1, 0)
        words[pl.ds(8 * n, 8), :] = jnp.where(k8 == 0, word, lax.population_count(word))
    t0 = pltpu.make_async_copy(table, table_s, sem_t.at[0])
    t1 = pltpu.make_async_copy(words, words_s, sem_t.at[1])
    t0.start()
    t1.start()
    t0.wait()
    t1.wait()

    def gather(p, total):
        for n in range(2):

            def one(m, bits):
                lowest = bits & -bits
                k = 31 - lax.clz(lowest) + 32 * n
                list_s[0, total + m] = table_s[k, p]
                list_s[1, total + m] = p
                return bits ^ lowest

            found = words_s[8 * n + 1, p]
            lax.fori_loop(0, found, one, words_s[8 * n, p])
            total = total + found
        return total

    def term(entry):
        a_at = pl.multiple_of((entry & 65535) * W, W)
        b_at = pl.multiple_of(lax.shift_right_logical(entry, 16) * W, W)
        a_high, a_low = split(a_all[pl.ds(a_at, W), :])
        b_high, b_low = split(b_all[pl.ds(b_at, W), :])
        left = jnp.concatenate([a_high, a_low], axis=1)
        right = jnp.concatenate(
            [jnp.concatenate([b_high, b_low], axis=1), jnp.concatenate([b_low, b_high], axis=1)], axis=0
        )
        both = jnp.dot(left, right, preferred_element_type=jnp.float32)
        return both[:, :W] + both[:, W:]

    def place(p):
        return pl.ds(pl.multiple_of(p // 8 * W, W), W), pl.ds(pl.multiple_of(p % 8 * W, W), W)

    total = lax.fori_loop(0, 32, gather, jnp.int32(0))
    settle(2)

    def four(t, _):
        terms = [term(list_s[0, 4 * t + n]) for n in range(4)]
        for n in range(4):
            rows, cols = place(list_s[1, 4 * t + n])
            acc[rows, cols] = acc[rows, cols] + terms[n]
        return 0

    def single(t, _):
        rows, cols = place(list_s[1, t])
        acc[rows, cols] = acc[rows, cols] + term(list_s[0, t])
        return 0

    lax.fori_loop(0, total // 4, four, 0)
    lax.fori_loop(total // 4 * 4, total, single, 0)
    out = pltpu.make_async_copy(acc, out_ref, sem_o)
    out.start()
    out.wait()


def product(spread, where, keep_tile, groups):
    hbm = pl.BlockSpec(memory_space=pl.ANY)
    shapes = tuple(len(group) for group in groups)
    pieces = [piece for group in groups for piece in group]
    more = (8, 16) if spread else (1, 1)
    return pl.pallas_call(
        functools.partial(product_kernel, shapes, spread),
        out_shape=jax.ShapeDtypeStruct((512, 1024), jnp.float32),
        in_specs=[pl.BlockSpec(memory_space=pltpu.SMEM), pl.BlockSpec(memory_space=pltpu.VMEM)] + [hbm] * len(pieces),
        out_specs=hbm,
        scratch_shapes=[
            pltpu.VMEM((512, 1024), jnp.float32),
            pltpu.VMEM(((8 + more[0]) * DATA, W), jnp.float32),
            pltpu.VMEM(((16 + more[1]) * DATA, W), jnp.float32),
            pltpu.VMEM((64, W), jnp.float32),
            pltpu.VMEM((128, W), jnp.float32),
            pltpu.VMEM((64, W), jnp.int32),
            pltpu.VMEM((16, W), jnp.int32),
            pltpu.SMEM((64, W), jnp.int32),
            pltpu.SMEM((16, W), jnp.int32),
            pltpu.SMEM((2, 2048), jnp.int32),
            pltpu.SemaphoreType.DMA((72,)),
            pltpu.SemaphoreType.DMA((2,)),
            pltpu.SemaphoreType.DMA,
        ],
        compiler_params=pltpu.CompilerParams(vmem_limit_bytes=(40 if spread else 24) * 1024 * 1024),
        name="product",
    )(where, keep_tile, *pieces)


def swap(x, axis):
    return lax.ppermute(x, axis, [(0, 1), (1, 0)])


def right(x, axis):
    return lax.ppermute(x, axis, [(n, (n + 1) % 4) for n in range(4)])


def left(x, axis):
    return lax.ppermute(x, axis, [(n, (n - 1) % 4) for n in range(4)])


def opposite(from_left, from_right, core, axis):
    if axis == "x":
        axes, at = ("core", "x"), lambda n, c: c * 4 + n % 4
    else:
        axes, at = ("y", "core"), lambda n, c: n % 4 * 2 + c
    pairs = [(at(n, c), at(n + 1 - 2 * c, c)) for n in range(4) for c in range(2)]
    return lax.ppermute(jnp.where(core == 0, from_left, from_right), axes, pairs)


def gate(*done):
    return lambda x: lax.optimization_barrier((x, *done))[0]


def around(own, z, axis, core):
    other = swap(own, z)
    found = []
    for x in (own, other):
        r, l = right(x, axis), left(x, axis)
        found.extend((x, r, l, opposite(r, l, core, axis)))
    return found


SIZES = (2, 4, 2, 2, 4)


def route(x, ring, z):
    pairs = []
    for n in range(128):
        zl, y, core, zh, at = (int(i) for i in np.unravel_index(n, SIZES))
        if core == 0:
            to = (zl, y, core, zh ^ z, ring(at))
        else:
            to = (zl ^ z, ring(y), core, zh, at)
        pairs.append((n, int(np.ravel_multi_index(to, SIZES))))
    return lax.ppermute(x, ROW + COL, pairs)


def forth(x):
    return route(x, lambda n: (n + 1) % 4, 0)


def back(x):
    return route(x, lambda n: (n - 1) % 4, 0)


def cross(x):
    return route(x, lambda n: n, 1)


def pair(x, distance):
    return route(x, lambda n: n ^ distance, 0)


def per_device(a_values, a_mask, b_values, b_mask, keep):
    zl, y, core = (lax.axis_index(n) for n in ROW)
    zh, x = (lax.axis_index(n) for n in COL)
    core_s = core.reshape(1).astype(jnp.int32)
    keep_tile = jnp.pad(jnp.transpose(keep, (1, 0, 2)).reshape(64, 32), ((0, 0), (0, W - 32)))
    held, sent = pack(core_s, a_mask, b_mask, a_values, b_values)
    m, e = merge(core_s, held, swap(sent, "core"))

    z0 = cross(m[:DATA])
    r, l = forth(m), back(m)
    e1 = pair(e, 1)
    cm = swap(m, "core")

    g = gate(r, l)
    z1 = cross(g(m[DATA:]))
    o0, o1 = forth(g(r[:DATA])), back(g(l[DATA:]))
    z0r, z0l = forth(g(z0)), back(g(z0))
    e = gate(o0, o1)(e) + e1
    e2 = pair(e, 2)
    cr, cl = swap(r, "core"), swap(l, "core")

    g = gate(z1, z0r, z0l)
    z1r, z1l = forth(g(z1)), back(g(z1))
    zo0 = forth((z0r))
    e = g(e) + e2
    e3 = cross(e)
    cz0, co0, co1 = swap(z0, "core"), swap(o0, "core"), swap(o1, "core")
    cz0r, cz0l = swap(z0r, "core"), swap(z0l, "core")

    g = gate(z1r, z1l, cm, cr, cl, co0, co1, cz0)
    zo1 = back(g(z1l))
    e = g(e) + e3
    cz1, cz1r, cz1l = swap(z1, "core"), swap(z1r, "core"), swap(z1l, "core")
    czo0 = swap(zo0, "core")
    ce = swap(e, "core")
    czo1 = swap(zo1, "core")

    shifts = (0, 3, 1, 2)
    groups = [[m], [cm], [r], [cr], [l], [cl], [o0, o1], [co0, co1]]
    groups += [[z0, z1], [cz0, cz1], [z0r, z1r], [cz0r, cz1r], [z0l, z1l], [cz0l, cz1l], [zo0, zo1], [czo0, czo1], [e, ce]]
    where = [core] + [(zh ^ n) * 4 + (x + s) % 4 for n in range(2) for s in shifts]
    where += [(zl ^ n) * 4 + (y + s) % 4 for n in range(2) for s in shifts]
    where = jnp.stack(where).astype(jnp.int32)
    crowd = [q[DATA, 0] > 1.5 for q in (e, ce)]

    def few(_):
        return product(False, where, keep_tile, groups)

    def many(_):
        first = core == 0
        crowd_a, crowd_b = jnp.where(first, crowd[0], crowd[1]), jnp.where(first, crowd[1], crowd[0])
        rest_a = jnp.where(first, held, sent)[DATA:TILES]
        rest_b = jnp.where(first, sent, held)[DATA:TILES]
        some_a = jnp.where(first, e, ce)[:DATA]
        some_b = jnp.where(first, ce, e)[:DATA]

        def all_b(_):
            found = around(rest_b, "zl", "y", core)
            return tuple(found + [swap(p, "core") for p in found])

        more = lax.cond(crowd_a, lambda _: tuple(around(rest_a, "zh", "x", core)), lambda _: (some_a,) * 8, 0)
        more += lax.cond(crowd_b, all_b, lambda _: (some_b,) * 16, 0)
        return product(True, where, keep_tile, groups + [[p] for p in more])

    return lax.cond(crowd[0] | crowd[1], many, few, 0)


def solution(mesh):
    fine = Mesh(mesh.devices.reshape(2, 4, 2, 2, 4), ROW + COL)
    return jax.shard_map(
        per_device,
        mesh=fine,
        in_specs=(P(ROW, COL), P(ROW, COL), P(ROW, COL), P(ROW, COL), P(ROW, None, COL)),
        out_specs=P(ROW, COL),
        check_vma=False,
    )
```

```python
import functools

import jax
import jax.numpy as jnp
import numpy as np
from jax import lax
from jax.experimental import pallas as pl
from jax.experimental.pallas import tpu as pltpu
from jax.sharding import Mesh
from jax.sharding import PartitionSpec as P

W = 128
SLOTS = 10
DATA = SLOTS * W
TILES = 2 * DATA
ROWS = TILES + 16
ROW = ("zl", "y", "core")
COL = ("zh", "x")


def pack_kernel(core_ref, am_ref, bm_ref, a_ref, b_ref, keep_ref, send_ref, sem):
    core = core_ref[0]
    row = lax.broadcasted_iota(jnp.int32, (8, W), 0)
    lane = lax.broadcasted_iota(jnp.int32, (8, W), 1)
    factors = (
        (am_ref, a_ref, lambda r, c: (row == c) & (lane // 8 == r)),
        (bm_ref, b_ref, lambda r, c: (row == r) & (lane % 8 == c)),
    )

    def copy(n, src, dst, r, c, cols, at):
        return pltpu.make_async_copy(
            src.at[pl.ds(r * W, W), pl.ds(c * W, W)], dst.at[pl.ds(at, W), :], sem.at[n * 32 + r * cols + c]
        )

    for n, (mask, src, spot) in enumerate(factors):
        rows, cols = mask.shape
        slot = jnp.int32(0)
        tile = jnp.zeros((8, W), jnp.float32)
        for r in range(rows):
            for c in range(cols):
                on = mask[r, c] != 0
                fits = on & (slot < 2 * SLOTS)
                at = pl.multiple_of(slot * W, W)
                for dst, here in ((keep_ref, core == n), (send_ref, core != n)):

                    @pl.when(fits & here)
                    def _():
                        copy(n, src, dst, r, c, cols, at).start()

                slot = slot + on.astype(jnp.int32)
                tile = jnp.where(spot(r, c), jnp.where(on, slot, 0).astype(jnp.float32), tile)
        flag = jnp.zeros((8, W), jnp.float32) + jnp.where(slot > SLOTS, 1.0, 0.0)
        for dst, here in ((keep_ref, core == n), (send_ref, core != n)):

            @pl.when(here)
            def _():
                dst[pl.ds(TILES, 8), :] = tile
                dst[pl.ds(TILES + 8, 8), :] = flag

    for n, (mask, src, _) in enumerate(factors):
        rows, cols = mask.shape
        for r in range(rows):
            for c in range(cols):

                @pl.when(mask[r, c] != 0)
                def _():
                    copy(n, src, keep_ref, r, c, cols, 0).wait()


def pack(core, a_mask, b_mask, a_values, b_values):
    smem = pl.BlockSpec(memory_space=pltpu.SMEM)
    vmem = pl.BlockSpec(memory_space=pltpu.VMEM)
    hbm = pl.BlockSpec(memory_space=pl.ANY)
    return pl.pallas_call(
        pack_kernel,
        out_shape=(jax.ShapeDtypeStruct((ROWS, W), jnp.float32),) * 2,
        in_specs=[smem, smem, smem, hbm, hbm],
        out_specs=(vmem,) * 2,
        scratch_shapes=[pltpu.SemaphoreType.DMA((64,))],
        name="pack",
    )(core, a_mask, b_mask, a_values, b_values)


def merge_kernel(core_ref, keep_ref, got_ref, main_ref, excess_ref):
    core = core_ref[0]
    for ref, at in ((keep_ref, core), (got_ref, 1 - core)):
        main_ref[pl.ds(pl.multiple_of(at * DATA, DATA), DATA), :] = ref[pl.ds(0, DATA), :]
        main_ref[pl.ds(pl.multiple_of(TILES + at * 8, 8), 8), :] = ref[pl.ds(TILES, 8), :]
    own = keep_ref[pl.ds(TILES + 8, 8), :]
    also = got_ref[pl.ds(TILES + 8, 8), :]
    kept = jnp.where(also[:1] > 0, got_ref[pl.ds(DATA, DATA), :], 0.0)
    excess_ref[pl.ds(0, DATA), :] = jnp.where(own[:1] > 0, keep_ref[pl.ds(DATA, DATA), :], kept)
    excess_ref[pl.ds(DATA, 8), :] = own + also


def merge(core, keep, got):
    vmem = pl.BlockSpec(memory_space=pltpu.VMEM)
    return pl.pallas_call(
        merge_kernel,
        out_shape=(
            jax.ShapeDtypeStruct((ROWS, W), jnp.float32),
            jax.ShapeDtypeStruct((DATA + 8, W), jnp.float32),
        ),
        in_specs=[pl.BlockSpec(memory_space=pltpu.SMEM), vmem, vmem],
        out_specs=(vmem, vmem),
        name="merge",
    )(core, keep, got)


def split(x):
    high = x.astype(jnp.bfloat16)
    low = (x - high.astype(jnp.float32)).astype(jnp.bfloat16)
    return high, low


def product_kernel(shapes, spread, where_ref, keep_ref, *refs):
    count = sum(shapes)
    pieces = list(refs[:count])
    out_ref, acc, a_all, b_all, a_meta, b_meta, table, words, table_s, words_s, list_s, sem, sem_t, sem_o = refs[count:]
    core = where_ref[0]
    groups = []
    for size in shapes:
        groups.append(pieces[:size])
        pieces = pieces[size:]
    lines, extra = groups[:17], groups[17:]

    def parts(piece):
        if len(piece) == 1:
            return [piece[0].at[pl.ds(0, DATA), :], piece[0].at[pl.ds(DATA, DATA), :], piece[0].at[pl.ds(TILES, 16), :]]
        return [piece[0], piece[1].at[pl.ds(0, DATA), :], piece[1].at[pl.ds(DATA, 16), :]]

    def copies(side):
        found = []
        for n in range(8):
            a_at, b_at = where_ref[1 + n], where_ref[9 + n]
            pair = (parts(lines[2 * n]), parts(lines[2 * n + 1]))
            a_parts, b_parts = pair[side], pair[1 - side]
            found.append((a_parts[side], a_all.at[pl.ds(a_at * DATA, DATA), :], 1 + n))
            found.append((a_parts[2].at[pl.ds(8 * side, 8), :], a_meta.at[pl.ds(a_at * 8, 8), :]))
            for h in range(2):
                found.append((b_parts[h], b_all.at[pl.ds((b_at * 2 + h) * DATA, DATA), :], 9 + n))
            found.append((b_parts[2], b_meta.at[pl.ds(b_at * 16, 16), :]))
        if not spread:
            e = lines[16]
            found.append((e[side].at[pl.ds(0, DATA), :], a_all.at[pl.ds(8 * DATA, DATA), :]))
            found.append((e[1 - side].at[pl.ds(0, DATA), :], b_all.at[pl.ds(16 * DATA, DATA), :]))
        for n, piece in enumerate(extra):
            if n < 8:
                found.append((piece[0], a_all.at[pl.ds((8 + where_ref[1 + n]) * DATA, DATA), :]))
            else:
                h = side if n < 16 else 1 - side
                at = 16 + where_ref[9 + n % 8] * 2 + h
                found.append((piece[0], b_all.at[pl.ds(at * DATA, DATA), :]))
        found.sort(key=lambda item: item[0].shape[0] >= DATA)
        made = []
        for n, item in enumerate(found):
            tag = item[2] if len(item) == 3 else (0 if item[0].shape[0] >= DATA else -1)
            made.append((pltpu.make_async_copy(item[0], item[1], sem.at[n]), tag))
        return made

    for side in range(2):

        @pl.when(core == side)
        def _():
            for copy, _ in copies(side):
                copy.start()

    def settle(half):
        for side in range(2):

            @pl.when(core == side)
            def _():
                for copy, tag in copies(side):
                    if tag > 0 and half >= 0:
                        pl.when(where_ref[tag] // 4 == half)(copy.wait)
                    elif (tag == 0 and half == 0) or (tag < 0 and half < 0):
                        copy.wait()

    acc[...] = jnp.zeros(acc.shape, jnp.float32)
    settle(-1)

    def address(piece, rank, pieces):
        rest = pieces * SLOTS + rank - (SLOTS + 1)
        if spread:
            rest = rest + piece * SLOTS
        return jnp.where(rank <= SLOTS, piece * SLOTS + rank - 1, rest)

    k8 = lax.broadcasted_iota(jnp.int32, (8, W), 0)
    one = jnp.ones((8, W), jnp.int32)
    low = jnp.zeros((8, W), jnp.int32)
    high = jnp.zeros((8, W), jnp.int32)
    for c in range(8):
        a_slot = a_meta[pl.ds(c * 8, 8), :].astype(jnp.int32)
        b0 = b_meta[pl.ds(c * 16, 8), :].astype(jnp.int32)
        b1 = pltpu.roll(b_meta[pl.ds(c * 16 + 8, 8), :], 4, 0).astype(jnp.int32)
        b_slot = jnp.where(k8 < 4, b0, b1)
        live = (keep_ref[pl.ds(c * 8, 8), :] != 0) & (a_slot > 0) & (b_slot > 0)
        a_at = address(c, a_slot, 8)
        b_at = address(jnp.where(k8 < 4, 2 * c, 2 * c + 1), b_slot, 16)
        table[pl.ds(c * 8, 8), :] = jnp.where(live, a_at + b_at * 65536, 0)
        bit = jnp.where(live, lax.shift_left(one, k8 + 8 * (c % 4)), 0)
        if c < 4:
            low = low | bit
        else:
            high = high | bit
    for n, word in enumerate((low, high)):
        word = word | pltpu.roll(word, 4, 0)
        word = word | pltpu.roll(word, 2, 0)
        word = word | pltpu.roll(word, 1, 0)
        words[pl.ds(8 * n, 8), :] = jnp.where(k8 == 0, word, lax.population_count(word))
    t0 = pltpu.make_async_copy(table, table_s, sem_t.at[0])
    t1 = pltpu.make_async_copy(words, words_s, sem_t.at[1])
    t0.start()
    t1.start()
    t0.wait()
    t1.wait()

    def gather(n, p, total):
        def one(m, bits):
            lowest = bits & -bits
            k = 31 - lax.clz(lowest) + 32 * n
            list_s[0, total + m] = table_s[k, p]
            list_s[1, total + m] = p
            return bits ^ lowest

        found = words_s[8 * n + 1, p]
        lax.fori_loop(0, found, one, words_s[8 * n, p])
        return total + found

    def term(entry):
        a_at = pl.multiple_of((entry & 65535) * W, W)
        b_at = pl.multiple_of(lax.shift_right_logical(entry, 16) * W, W)
        a_high, a_low = split(a_all[pl.ds(a_at, W), :])
        b_high, b_low = split(b_all[pl.ds(b_at, W), :])
        left = jnp.concatenate([a_high, a_low], axis=1)
        right = jnp.concatenate(
            [jnp.concatenate([b_high, b_low], axis=1), jnp.concatenate([b_low, b_high], axis=1)], axis=0
        )
        both = jnp.dot(left, right, preferred_element_type=jnp.float32)
        return both[:, :W] + both[:, W:]

    def place(p):
        return pl.ds(pl.multiple_of(p // 8 * W, W), W), pl.ds(pl.multiple_of(p % 8 * W, W), W)

    begin = jnp.int32(0)
    middle = lax.fori_loop(0, 32, functools.partial(gather, 0), begin)
    end = lax.fori_loop(0, 32, functools.partial(gather, 1), middle)

    def add(n, value):
        rows, cols = place(list_s[1, n])
        acc[rows, cols] = acc[rows, cols] + value

    for half, (start, stop) in enumerate(((begin, middle), (middle, end))):
        settle(half)
        fours = (stop - start) // 4

        def four(t, start):
            at = start + 4 * t
            terms = [term(list_s[0, at + n]) for n in range(4)]
            for n in range(4):
                add(at + n, terms[n])
            return start

        def single(t, _):
            add(t, term(list_s[0, t]))
            return 0

        lax.fori_loop(0, fours, four, start)
        lax.fori_loop(start + 4 * fours, stop, single, 0)
    out = pltpu.make_async_copy(acc, out_ref, sem_o)
    out.start()
    out.wait()


def product(spread, where, keep_tile, groups):
    hbm = pl.BlockSpec(memory_space=pl.ANY)
    shapes = tuple(len(group) for group in groups)
    pieces = [piece for group in groups for piece in group]
    more = (8, 16) if spread else (1, 1)
    return pl.pallas_call(
        functools.partial(product_kernel, shapes, spread),
        out_shape=jax.ShapeDtypeStruct((512, 1024), jnp.float32),
        in_specs=[pl.BlockSpec(memory_space=pltpu.SMEM), pl.BlockSpec(memory_space=pltpu.VMEM)] + [hbm] * len(pieces),
        out_specs=hbm,
        scratch_shapes=[
            pltpu.VMEM((512, 1024), jnp.float32),
            pltpu.VMEM(((8 + more[0]) * DATA, W), jnp.float32),
            pltpu.VMEM(((16 + more[1]) * DATA, W), jnp.float32),
            pltpu.VMEM((64, W), jnp.float32),
            pltpu.VMEM((128, W), jnp.float32),
            pltpu.VMEM((64, W), jnp.int32),
            pltpu.VMEM((16, W), jnp.int32),
            pltpu.SMEM((64, W), jnp.int32),
            pltpu.SMEM((16, W), jnp.int32),
            pltpu.SMEM((2, 2048), jnp.int32),
            pltpu.SemaphoreType.DMA((72,)),
            pltpu.SemaphoreType.DMA((2,)),
            pltpu.SemaphoreType.DMA,
        ],
        compiler_params=pltpu.CompilerParams(vmem_limit_bytes=(40 if spread else 24) * 1024 * 1024),
        name="product",
    )(where, keep_tile, *pieces)


def swap(x, axis):
    return lax.ppermute(x, axis, [(0, 1), (1, 0)])


def right(x, axis):
    return lax.ppermute(x, axis, [(n, (n + 1) % 4) for n in range(4)])


def left(x, axis):
    return lax.ppermute(x, axis, [(n, (n - 1) % 4) for n in range(4)])


def opposite(from_left, from_right, core, axis):
    if axis == "x":
        axes, at = ("core", "x"), lambda n, c: c * 4 + n % 4
    else:
        axes, at = ("y", "core"), lambda n, c: n % 4 * 2 + c
    pairs = [(at(n, c), at(n + 1 - 2 * c, c)) for n in range(4) for c in range(2)]
    return lax.ppermute(jnp.where(core == 0, from_left, from_right), axes, pairs)


def gate(*done):
    return lambda x: lax.optimization_barrier((x, *done))[0]


def around(own, z, axis, core):
    other = swap(own, z)
    found = []
    for x in (own, other):
        r, l = right(x, axis), left(x, axis)
        found.extend((x, r, l, opposite(r, l, core, axis)))
    return found


SIZES = (2, 4, 2, 2, 4)


def route(x, ring, z):
    pairs = []
    for n in range(128):
        zl, y, core, zh, at = (int(i) for i in np.unravel_index(n, SIZES))
        if core == 0:
            to = (zl, y, core, zh ^ z, ring(at))
        else:
            to = (zl ^ z, ring(y), core, zh, at)
        pairs.append((n, int(np.ravel_multi_index(to, SIZES))))
    return lax.ppermute(x, ROW + COL, pairs)


def forth(x):
    return route(x, lambda n: (n + 1) % 4, 0)


def back(x):
    return route(x, lambda n: (n - 1) % 4, 0)


def cross(x):
    return route(x, lambda n: n, 1)


def pair(x, distance):
    return route(x, lambda n: n ^ distance, 0)


def per_device(a_values, a_mask, b_values, b_mask, keep):
    zl, y, core = (lax.axis_index(n) for n in ROW)
    zh, x = (lax.axis_index(n) for n in COL)
    core_s = core.reshape(1).astype(jnp.int32)
    keep_tile = jnp.pad(jnp.transpose(keep, (1, 0, 2)).reshape(64, 32), ((0, 0), (0, W - 32)))
    held, sent = pack(core_s, a_mask, b_mask, a_values, b_values)
    m, e = merge(core_s, held, swap(sent, "core"))

    z0 = cross(m[:DATA])
    r, l = forth(m), back(m)
    e1 = pair(e, 1)
    cm = swap(m, "core")

    g = gate(r, l)
    z1 = cross(g(m[DATA:]))
    o0, o1 = forth(g(r[:DATA])), back(g(l[DATA:]))
    z0r, z0l = forth(g(z0)), back(g(z0))
    e = gate(o0, o1)(e) + e1
    e2 = pair(e, 2)
    cr, cl = swap(r, "core"), swap(l, "core")

    g = gate(z1, z0r, z0l)
    z1r, z1l = forth(g(z1)), back(g(z1))
    zo0 = forth((z0r))
    e = g(e) + e2
    e3 = cross(e)
    cz0, co0, co1 = swap(z0, "core"), swap(o0, "core"), swap(o1, "core")
    cz0r, cz0l = swap(z0r, "core"), swap(z0l, "core")

    g = gate(z1r, z1l, cm, cr, cl, co0, co1, cz0)
    zo1 = back(g(z1l))
    e = g(e) + e3
    cz1, cz1r, cz1l = swap(z1, "core"), swap(z1r, "core"), swap(z1l, "core")
    czo0 = swap(zo0, "core")
    ce = swap(e, "core")
    czo1 = swap(zo1, "core")

    shifts = (0, 3, 1, 2)
    groups = [[m], [cm], [r], [cr], [l], [cl], [o0, o1], [co0, co1]]
    groups += [[z0, z1], [cz0, cz1], [z0r, z1r], [cz0r, cz1r], [z0l, z1l], [cz0l, cz1l], [zo0, zo1], [czo0, czo1], [e, ce]]
    where = [core] + [(zh ^ n) * 4 + (x + s) % 4 for n in range(2) for s in shifts]
    where += [(zl ^ n) * 4 + (y + s) % 4 for n in range(2) for s in shifts]
    where = jnp.stack(where).astype(jnp.int32)
    crowd = [q[DATA, 0] > 1.5 for q in (e, ce)]

    def few(_):
        return product(False, where, keep_tile, groups)

    def many(_):
        first = core == 0
        crowd_a, crowd_b = jnp.where(first, crowd[0], crowd[1]), jnp.where(first, crowd[1], crowd[0])
        rest_a = jnp.where(first, held, sent)[DATA:TILES]
        rest_b = jnp.where(first, sent, held)[DATA:TILES]
        some_a = jnp.where(first, e, ce)[:DATA]
        some_b = jnp.where(first, ce, e)[:DATA]

        def all_b(_):
            found = around(rest_b, "zl", "y", core)
            return tuple(found + [swap(p, "core") for p in found])

        more = lax.cond(crowd_a, lambda _: tuple(around(rest_a, "zh", "x", core)), lambda _: (some_a,) * 8, 0)
        more += lax.cond(crowd_b, all_b, lambda _: (some_b,) * 16, 0)
        return product(True, where, keep_tile, groups + [[p] for p in more])

    return lax.cond(crowd[0] | crowd[1], many, few, 0)


def solution(mesh):
    fine = Mesh(mesh.devices.reshape(2, 4, 2, 2, 4), ROW + COL)
    return jax.shard_map(
        per_device,
        mesh=fine,
        in_specs=(P(ROW, COL), P(ROW, COL), P(ROW, COL), P(ROW, COL), P(ROW, None, COL)),
        out_specs=P(ROW, COL),
        check_vma=False,
    )
```

```python
import functools

import jax
import jax.numpy as jnp
import numpy as np
from jax import lax
from jax.experimental import pallas as pl
from jax.experimental.pallas import tpu as pltpu
from jax.sharding import Mesh
from jax.sharding import PartitionSpec as P

W = 128
SLOTS = 10
DATA = SLOTS * W
TILES = 2 * DATA
ROWS = TILES + 16
ROW = ("zl", "y", "core")
COL = ("zh", "x")


def pack_kernel(core_ref, am_ref, bm_ref, a_ref, b_ref, keep_ref, send_ref, sem):
    core = core_ref[0]
    row = lax.broadcasted_iota(jnp.int32, (8, W), 0)
    lane = lax.broadcasted_iota(jnp.int32, (8, W), 1)
    factors = (
        (am_ref, a_ref, lambda r, c: (row == c) & (lane // 8 == r)),
        (bm_ref, b_ref, lambda r, c: (row == r) & (lane % 8 == c)),
    )

    def copy(n, src, dst, r, c, cols, at):
        return pltpu.make_async_copy(
            src.at[pl.ds(r * W, W), pl.ds(c * W, W)], dst.at[pl.ds(at, W), :], sem.at[n * 32 + r * cols + c]
        )

    for n, (mask, src, spot) in enumerate(factors):
        rows, cols = mask.shape
        slot = jnp.int32(0)
        tile = jnp.zeros((8, W), jnp.float32)
        for r in range(rows):
            for c in range(cols):
                on = mask[r, c] != 0
                fits = on & (slot < 2 * SLOTS)
                at = pl.multiple_of(slot * W, W)
                for dst, here in ((keep_ref, core == n), (send_ref, core != n)):

                    @pl.when(fits & here)
                    def _():
                        copy(n, src, dst, r, c, cols, at).start()

                slot = slot + on.astype(jnp.int32)
                tile = jnp.where(spot(r, c), jnp.where(on, slot, 0).astype(jnp.float32), tile)
        flag = jnp.zeros((8, W), jnp.float32) + jnp.where(slot > SLOTS, 1.0, 0.0)
        for dst, here in ((keep_ref, core == n), (send_ref, core != n)):

            @pl.when(here)
            def _():
                dst[pl.ds(TILES, 8), :] = tile
                dst[pl.ds(TILES + 8, 8), :] = flag

    for n, (mask, src, _) in enumerate(factors):
        rows, cols = mask.shape
        for r in range(rows):
            for c in range(cols):

                @pl.when(mask[r, c] != 0)
                def _():
                    copy(n, src, keep_ref, r, c, cols, 0).wait()


def pack(core, a_mask, b_mask, a_values, b_values):
    smem = pl.BlockSpec(memory_space=pltpu.SMEM)
    vmem = pl.BlockSpec(memory_space=pltpu.VMEM)
    hbm = pl.BlockSpec(memory_space=pl.ANY)
    return pl.pallas_call(
        pack_kernel,
        out_shape=(jax.ShapeDtypeStruct((ROWS, W), jnp.float32),) * 2,
        in_specs=[smem, smem, smem, hbm, hbm],
        out_specs=(vmem,) * 2,
        scratch_shapes=[pltpu.SemaphoreType.DMA((64,))],
        name="pack",
    )(core, a_mask, b_mask, a_values, b_values)


def merge_kernel(core_ref, keep_ref, got_ref, main_ref, excess_ref):
    core = core_ref[0]
    for ref, at in ((keep_ref, core), (got_ref, 1 - core)):
        main_ref[pl.ds(pl.multiple_of(at * DATA, DATA), DATA), :] = ref[pl.ds(0, DATA), :]
        main_ref[pl.ds(pl.multiple_of(TILES + at * 8, 8), 8), :] = ref[pl.ds(TILES, 8), :]
    own = keep_ref[pl.ds(TILES + 8, 8), :]
    also = got_ref[pl.ds(TILES + 8, 8), :]
    kept = jnp.where(also[:1] > 0, got_ref[pl.ds(DATA, DATA), :], 0.0)
    excess_ref[pl.ds(0, DATA), :] = jnp.where(own[:1] > 0, keep_ref[pl.ds(DATA, DATA), :], kept)
    excess_ref[pl.ds(DATA, 8), :] = own + also


def merge(core, keep, got):
    vmem = pl.BlockSpec(memory_space=pltpu.VMEM)
    return pl.pallas_call(
        merge_kernel,
        out_shape=(
            jax.ShapeDtypeStruct((ROWS, W), jnp.float32),
            jax.ShapeDtypeStruct((DATA + 8, W), jnp.float32),
        ),
        in_specs=[pl.BlockSpec(memory_space=pltpu.SMEM), vmem, vmem],
        out_specs=(vmem, vmem),
        name="merge",
    )(core, keep, got)


def split(x):
    high = x.astype(jnp.bfloat16)
    low = (x - high.astype(jnp.float32)).astype(jnp.bfloat16)
    return high, low


def product_kernel(shapes, spread, where_ref, keep_ref, *refs):
    count = sum(shapes)
    pieces = list(refs[:count])
    out_ref, acc, a_all, b_all, a_meta, b_meta, table, words, table_s, words_s, list_s, sem, sem_t, sem_o = refs[count:]
    core = where_ref[0]
    groups = []
    for size in shapes:
        groups.append(pieces[:size])
        pieces = pieces[size:]
    lines, extra = groups[:17], groups[17:]

    def parts(piece):
        if len(piece) == 1:
            return [piece[0].at[pl.ds(0, DATA), :], piece[0].at[pl.ds(DATA, DATA), :], piece[0].at[pl.ds(TILES, 16), :]]
        return [piece[0], piece[1].at[pl.ds(0, DATA), :], piece[1].at[pl.ds(DATA, 16), :]]

    def copies(side):
        found = []
        for n in range(8):
            a_at, b_at = where_ref[1 + n], where_ref[9 + n]
            pair = (parts(lines[2 * n]), parts(lines[2 * n + 1]))
            a_parts, b_parts = pair[side], pair[1 - side]
            found.append((a_parts[side], a_all.at[pl.ds(a_at * DATA, DATA), :], 1 + n))
            found.append((a_parts[2].at[pl.ds(8 * side, 8), :], a_meta.at[pl.ds(a_at * 8, 8), :]))
            for h in range(2):
                found.append((b_parts[h], b_all.at[pl.ds((b_at * 2 + h) * DATA, DATA), :], 9 + n))
            found.append((b_parts[2], b_meta.at[pl.ds(b_at * 16, 16), :]))
        if not spread:
            e = lines[16]
            found.append((e[side].at[pl.ds(0, DATA), :], a_all.at[pl.ds(8 * DATA, DATA), :]))
            found.append((e[1 - side].at[pl.ds(0, DATA), :], b_all.at[pl.ds(16 * DATA, DATA), :]))
        for n, piece in enumerate(extra):
            if n < 8:
                found.append((piece[0], a_all.at[pl.ds((8 + where_ref[1 + n]) * DATA, DATA), :]))
            else:
                h = side if n < 16 else 1 - side
                at = 16 + where_ref[9 + n % 8] * 2 + h
                found.append((piece[0], b_all.at[pl.ds(at * DATA, DATA), :]))
        found.sort(key=lambda item: item[0].shape[0] >= DATA)
        made = []
        for n, item in enumerate(found):
            tag = item[2] if len(item) == 3 else (0 if item[0].shape[0] >= DATA else -1)
            made.append((pltpu.make_async_copy(item[0], item[1], sem.at[n]), tag))
        return made

    for side in range(2):

        @pl.when(core == side)
        def _():
            for copy, _ in copies(side):
                copy.start()

    def settle(half):
        for side in range(2):

            @pl.when(core == side)
            def _():
                for copy, tag in copies(side):
                    if tag > 0 and half >= 0:
                        pl.when(where_ref[tag] // 4 == half)(copy.wait)
                    elif (tag == 0 and half == 0) or (tag < 0 and half < 0):
                        copy.wait()

    acc[...] = jnp.zeros(acc.shape, jnp.float32)
    settle(-1)

    def address(piece, rank, pieces):
        rest = pieces * SLOTS + rank - (SLOTS + 1)
        if spread:
            rest = rest + piece * SLOTS
        return jnp.where(rank <= SLOTS, piece * SLOTS + rank - 1, rest)

    k8 = lax.broadcasted_iota(jnp.int32, (8, W), 0)
    one = jnp.ones((8, W), jnp.int32)
    low = jnp.zeros((8, W), jnp.int32)
    high = jnp.zeros((8, W), jnp.int32)
    for c in range(8):
        a_slot = a_meta[pl.ds(c * 8, 8), :].astype(jnp.int32)
        b0 = b_meta[pl.ds(c * 16, 8), :].astype(jnp.int32)
        b1 = pltpu.roll(b_meta[pl.ds(c * 16 + 8, 8), :], 4, 0).astype(jnp.int32)
        b_slot = jnp.where(k8 < 4, b0, b1)
        live = (keep_ref[pl.ds(c * 8, 8), :] != 0) & (a_slot > 0) & (b_slot > 0)
        a_at = address(c, a_slot, 8)
        b_at = address(jnp.where(k8 < 4, 2 * c, 2 * c + 1), b_slot, 16)
        table[pl.ds(c * 8, 8), :] = jnp.where(live, a_at + b_at * 65536, 0)
        bit = jnp.where(live, lax.shift_left(one, k8 + 8 * (c % 4)), 0)
        if c < 4:
            low = low | bit
        else:
            high = high | bit
    for n, word in enumerate((low, high)):
        word = word | pltpu.roll(word, 4, 0)
        word = word | pltpu.roll(word, 2, 0)
        word = word | pltpu.roll(word, 1, 0)
        words[pl.ds(8 * n, 8), :] = jnp.where(k8 == 0, word, lax.population_count(word))
    t0 = pltpu.make_async_copy(table, table_s, sem_t.at[0])
    t1 = pltpu.make_async_copy(words, words_s, sem_t.at[1])
    t0.start()
    t1.start()
    t0.wait()
    t1.wait()

    def gather(n, p, total):
        def one(m, bits):
            lowest = bits & -bits
            k = 31 - lax.clz(lowest) + 32 * n
            list_s[0, total + m] = table_s[k, p]
            list_s[1, total + m] = p
            return bits ^ lowest

        found = words_s[8 * n + 1, p]
        lax.fori_loop(0, found, one, words_s[8 * n, p])
        return total + found

    def term(entry):
        a_at = pl.multiple_of((entry & 65535) * W, W)
        b_at = pl.multiple_of(lax.shift_right_logical(entry, 16) * W, W)
        a_high, a_low = split(a_all[pl.ds(a_at, W), :])
        b_high, b_low = split(b_all[pl.ds(b_at, W), :])
        left = jnp.concatenate([a_high, a_low], axis=1)
        right = jnp.concatenate(
            [jnp.concatenate([b_high, b_low], axis=1), jnp.concatenate([b_low, b_high], axis=1)], axis=0
        )
        both = jnp.dot(left, right, preferred_element_type=jnp.float32)
        return both[:, :W] + both[:, W:]

    def place(p):
        return pl.ds(pl.multiple_of(p // 8 * W, W), W), pl.ds(pl.multiple_of(p % 8 * W, W), W)

    begin = jnp.int32(0)
    middle = lax.fori_loop(0, 32, functools.partial(gather, 0), begin)
    end = lax.fori_loop(0, 32, functools.partial(gather, 1), middle)

    def add(n, value):
        rows, cols = place(list_s[1, n])
        acc[rows, cols] = acc[rows, cols] + value

    for half, (start, stop) in enumerate(((begin, middle), (middle, end))):
        settle(half)
        def several(width, t, start):
            at = start + width * t
            terms = [term(list_s[0, at + n]) for n in range(width)]
            for n in range(width):
                add(at + n, terms[n])
            return start

        def single(t, _):
            add(t, term(list_s[0, t]))
            return 0

        for width in (8, 4):
            times = (stop - start) // width
            lax.fori_loop(0, times, functools.partial(several, width), start)
            start = start + width * times
        lax.fori_loop(start, stop, single, 0)
    out = pltpu.make_async_copy(acc, out_ref, sem_o)
    out.start()
    out.wait()


def product(spread, where, keep_tile, groups):
    hbm = pl.BlockSpec(memory_space=pl.ANY)
    shapes = tuple(len(group) for group in groups)
    pieces = [piece for group in groups for piece in group]
    more = (8, 16) if spread else (1, 1)
    return pl.pallas_call(
        functools.partial(product_kernel, shapes, spread),
        out_shape=jax.ShapeDtypeStruct((512, 1024), jnp.float32),
        in_specs=[pl.BlockSpec(memory_space=pltpu.SMEM), pl.BlockSpec(memory_space=pltpu.VMEM)] + [hbm] * len(pieces),
        out_specs=hbm,
        scratch_shapes=[
            pltpu.VMEM((512, 1024), jnp.float32),
            pltpu.VMEM(((8 + more[0]) * DATA, W), jnp.float32),
            pltpu.VMEM(((16 + more[1]) * DATA, W), jnp.float32),
            pltpu.VMEM((64, W), jnp.float32),
            pltpu.VMEM((128, W), jnp.float32),
            pltpu.VMEM((64, W), jnp.int32),
            pltpu.VMEM((16, W), jnp.int32),
            pltpu.SMEM((64, W), jnp.int32),
            pltpu.SMEM((16, W), jnp.int32),
            pltpu.SMEM((2, 2048), jnp.int32),
            pltpu.SemaphoreType.DMA((72,)),
            pltpu.SemaphoreType.DMA((2,)),
            pltpu.SemaphoreType.DMA,
        ],
        compiler_params=pltpu.CompilerParams(vmem_limit_bytes=(40 if spread else 24) * 1024 * 1024),
        name="product",
    )(where, keep_tile, *pieces)


def swap(x, axis):
    return lax.ppermute(x, axis, [(0, 1), (1, 0)])


def right(x, axis):
    return lax.ppermute(x, axis, [(n, (n + 1) % 4) for n in range(4)])


def left(x, axis):
    return lax.ppermute(x, axis, [(n, (n - 1) % 4) for n in range(4)])


def opposite(from_left, from_right, core, axis):
    if axis == "x":
        axes, at = ("core", "x"), lambda n, c: c * 4 + n % 4
    else:
        axes, at = ("y", "core"), lambda n, c: n % 4 * 2 + c
    pairs = [(at(n, c), at(n + 1 - 2 * c, c)) for n in range(4) for c in range(2)]
    return lax.ppermute(jnp.where(core == 0, from_left, from_right), axes, pairs)


def gate(*done):
    return lambda x: lax.optimization_barrier((x, *done))[0]


def around(own, z, axis, core):
    other = swap(own, z)
    found = []
    for x in (own, other):
        r, l = right(x, axis), left(x, axis)
        found.extend((x, r, l, opposite(r, l, core, axis)))
    return found


SIZES = (2, 4, 2, 2, 4)


def route(x, ring, z):
    pairs = []
    for n in range(128):
        zl, y, core, zh, at = (int(i) for i in np.unravel_index(n, SIZES))
        if core == 0:
            to = (zl, y, core, zh ^ z, ring(at))
        else:
            to = (zl ^ z, ring(y), core, zh, at)
        pairs.append((n, int(np.ravel_multi_index(to, SIZES))))
    return lax.ppermute(x, ROW + COL, pairs)


def forth(x):
    return route(x, lambda n: (n + 1) % 4, 0)


def back(x):
    return route(x, lambda n: (n - 1) % 4, 0)


def cross(x):
    return route(x, lambda n: n, 1)


def pair(x, distance):
    return route(x, lambda n: n ^ distance, 0)


def per_device(a_values, a_mask, b_values, b_mask, keep):
    zl, y, core = (lax.axis_index(n) for n in ROW)
    zh, x = (lax.axis_index(n) for n in COL)
    core_s = core.reshape(1).astype(jnp.int32)
    keep_tile = jnp.pad(jnp.transpose(keep, (1, 0, 2)).reshape(64, 32), ((0, 0), (0, W - 32)))
    held, sent = pack(core_s, a_mask, b_mask, a_values, b_values)
    m, e = merge(core_s, held, swap(sent, "core"))

    z0 = cross(m[:DATA])
    r, l = forth(m), back(m)
    e1 = pair(e, 1)
    cm = swap(m, "core")

    g = gate(r, l)
    z1 = cross(g(m[DATA:]))
    o0, o1 = forth(g(r[:DATA])), back(g(l[DATA:]))
    z0r, z0l = forth(g(z0)), back(g(z0))
    e = gate(o0, o1)(e) + e1
    e2 = pair(e, 2)
    cr, cl = swap(r, "core"), swap(l, "core")

    g = gate(z1, z0r, z0l)
    z1r, z1l = forth(g(z1)), back(g(z1))
    zo0 = forth((z0r))
    e = g(e) + e2
    e3 = cross(e)
    cz0, co0, co1 = swap(z0, "core"), swap(o0, "core"), swap(o1, "core")
    cz0r, cz0l = swap(z0r, "core"), swap(z0l, "core")

    g = gate(z1r, z1l, cm, cr, cl, co0, co1, cz0)
    zo1 = back(g(z1l))
    e = g(e) + e3
    cz1, cz1r, cz1l = swap(z1, "core"), swap(z1r, "core"), swap(z1l, "core")
    czo0 = swap(zo0, "core")
    ce = swap(e, "core")
    czo1 = swap(zo1, "core")

    shifts = (0, 3, 1, 2)
    groups = [[m], [cm], [r], [cr], [l], [cl], [o0, o1], [co0, co1]]
    groups += [[z0, z1], [cz0, cz1], [z0r, z1r], [cz0r, cz1r], [z0l, z1l], [cz0l, cz1l], [zo0, zo1], [czo0, czo1], [e, ce]]
    where = [core] + [(zh ^ n) * 4 + (x + s) % 4 for n in range(2) for s in shifts]
    where += [(zl ^ n) * 4 + (y + s) % 4 for n in range(2) for s in shifts]
    where = jnp.stack(where).astype(jnp.int32)
    crowd = [q[DATA, 0] > 1.5 for q in (e, ce)]

    def few(_):
        return product(False, where, keep_tile, groups)

    def many(_):
        first = core == 0
        crowd_a, crowd_b = jnp.where(first, crowd[0], crowd[1]), jnp.where(first, crowd[1], crowd[0])
        rest_a = jnp.where(first, held, sent)[DATA:TILES]
        rest_b = jnp.where(first, sent, held)[DATA:TILES]
        some_a = jnp.where(first, e, ce)[:DATA]
        some_b = jnp.where(first, ce, e)[:DATA]

        def all_b(_):
            found = around(rest_b, "zl", "y", core)
            return tuple(found + [swap(p, "core") for p in found])

        more = lax.cond(crowd_a, lambda _: tuple(around(rest_a, "zh", "x", core)), lambda _: (some_a,) * 8, 0)
        more += lax.cond(crowd_b, all_b, lambda _: (some_b,) * 16, 0)
        return product(True, where, keep_tile, groups + [[p] for p in more])

    return lax.cond(crowd[0] | crowd[1], many, few, 0)


def solution(mesh):
    fine = Mesh(mesh.devices.reshape(2, 4, 2, 2, 4), ROW + COL)
    return jax.shard_map(
        per_device,
        mesh=fine,
        in_specs=(P(ROW, COL), P(ROW, COL), P(ROW, COL), P(ROW, COL), P(ROW, None, COL)),
        out_specs=P(ROW, COL),
        check_vma=False,
    )
```
